512 devices in a mesh: frame: 64 (over x, z, core), head: 8 (over y).
Axes of the slice: x: 4, y: 8, z: 8, core: 2. Of those that a mesh axis runs over, the one named last changes fastest.
Arguments:
- tokens: bfloat16 [8192, 5120], P('frame'), may hold values from -6 to 6
- w_query: bfloat16 [5120, 3072], P('frame', 'head')
- w_key: bfloat16 [5120, 3072], P('frame', 'head')
- w_value: bfloat16 [5120, 3072], P('frame', 'head'), may hold values from -0.078125 to 0.078125
- query_gain: float32 [3072], P('head')
- key_gain: float32 [3072], P('head')
- key_tiles: int32 [64, 12], replicated, may hold values from -1 to 63, as said below
Outputs:
- attended: bfloat16 [8192, 3072], P('frame', 'head')
The draws below stay inside these ranges and needn't reach their ends.
Inputs may be any that keep to these rules, and one draw needn't show every extreme that they name: Each frame index holds exactly one query tile, so tile t lives on frame index t. Row t of key_tiles names distinct key tiles first and is padded with -1 after them. A named tile u has u - t in 0, 1, -1, 2, -2 or plus or minus a power of two from 4 up to half the number of frame devices, and every tile with u - t in 0, 1, -1 that exists is named.
All inputs are finite; a program needn't handle non-finite values.
Results may differ from the reference program's by a relative error of at most 0.028.
Values may be sent and summed in bfloat16 or wider, within the bound.
No kernel may reach another device: no remote copies, remote signals or barrier semaphores. Data moves between devices by JAX's collectives and lax.ppermute only.
A program may use at most 64 MiB of HBM per device.

```python
import math
import jax
import jax.numpy as jnp
from jax import lax

D = 5120
HEAD_DIM = 128
HEADS = 24
TILE = 128
TOK_DEV = 128
TOKENS = 8192
LIST = 12
N_FRAME = 64


def projection_pair(key):
    width = HEADS * HEAD_DIM
    head_of = jnp.arange(width) // HEAD_DIM
    ramp = 3.0 ** (head_of.astype(jnp.float32) / max(HEADS - 1, 1))
    rough_query = jnp.exp(jax.random.uniform(jax.random.fold_in(key, 7), (width,), jnp.float32, 0.0, math.log(10.0)))
    rough_key = jnp.exp(jax.random.uniform(jax.random.fold_in(key, 8), (width,), jnp.float32, 0.0, math.log(10.0)))
    base_query = jax.random.normal(jax.random.fold_in(key, 5), (D, width), jnp.float32) * D ** (-0.5)
    base_key = jax.random.normal(jax.random.fold_in(key, 6), (D, width), jnp.float32) * D ** (-0.5)
    base_query = base_query * (ramp * rough_query / 6.0)[None, :]
    base_key = base_key * (ramp * rough_key / 6.0)[None, :]
    return (base_query, base_key)


def draw_w_query(key, part):
    return projection_pair(key)[0].astype(jnp.bfloat16)


def draw_w_key(key, part):
    return projection_pair(key)[1].astype(jnp.bfloat16)


def gain_values(key):
    width = HEADS * HEAD_DIM
    return jnp.exp(jax.random.uniform(key, (width,), jnp.float32, math.log(0.5), math.log(2.0)))


def draw_query_gain(key, part):
    return gain_values(jax.random.fold_in(key, 31))


def draw_key_gain(key, part):
    return gain_values(jax.random.fold_in(key, 32))


def draw_key_tiles(key, part):
    tiles_per = TOK_DEV // TILE
    all_tiles = N_FRAME * tiles_per
    query_index = jnp.arange(all_tiles, dtype=jnp.int32)
    owner = query_index // tiles_per
    local_tiles = jnp.arange(tiles_per, dtype=jnp.int32)
    forced = query_index == N_FRAME // 2 * tiles_per
    tile_ids = []
    keep_flags = []
    for offset in (0, -1, 1):
        target = owner + offset
        inside = (target >= 0) & (target < N_FRAME)
        tile_ids.append(target[:, None] * tiles_per + local_tiles[None, :])
        keep_flags.append(jnp.broadcast_to(inside[:, None], (all_tiles, tiles_per)))
    for number, offset in enumerate((-2, 2)):
        target = owner + offset
        inside = (target >= 0) & (target < N_FRAME)
        coin_flip = jax.random.randint(jax.random.fold_in(key, 20 + number), (all_tiles, tiles_per), 0, 2)
        tile_ids.append(target[:, None] * tiles_per + local_tiles[None, :])
        keep_flags.append(inside[:, None] & ((coin_flip == 0) | forced[:, None]))
    stride = 4
    level_number = 2
    while stride <= N_FRAME // 2:
        for direction in (-1, 1):
            offset = direction * stride
            target = owner + offset
            inside = (target >= 0) & (target < N_FRAME)
            salt = 4 * level_number + (direction + 1) // 2
            chosen_tile = jax.random.randint(jax.random.fold_in(key, 100 + salt), (N_FRAME,), 0, tiles_per)
            coin_flip = jax.random.randint(jax.random.fold_in(key, 300 + salt), (all_tiles,), 0, stride // 2)
            tile_ids.append((target * tiles_per + chosen_tile[owner])[:, None])
            keep_flags.append((inside & ((coin_flip == 0) | forced))[:, None])
        stride = stride * 2
        level_number = level_number + 1
    tile_all = jnp.concatenate(tile_ids, axis=1).astype(jnp.int32)
    keep_all = jnp.concatenate(keep_flags, axis=1)
    entries = jnp.where(keep_all, tile_all, -1)
    positions = jnp.arange(tile_all.shape[1], dtype=jnp.int32)
    order_key = jnp.where(keep_all, 0, 1) * 100000 + positions[None, :]
    order = jnp.argsort(order_key, axis=1, stable=True)
    return jnp.take_along_axis(entries, order, axis=1)[:, :LIST].astype(jnp.int32)


def block_levels(stream_key, shape, cuts, low, high):
    def one(axis_at, parts):
        draws = jax.random.uniform(jax.random.fold_in(jax.random.fold_in(stream_key, 6), axis_at), (parts,), jnp.float32, low / len(cuts), high / len(cuts))
        return jnp.repeat(jnp.exp(draws), shape[axis_at] // parts).reshape((-1,) + (1,) * (len(shape) - axis_at - 1))

    level = one(*cuts[0])
    for cut in cuts[1:]:
        level = level * one(*cut)
    return level


def centred(stream_key, shape, spread, bound, pieces=(), kind=jnp.bfloat16):
    level = block_levels(stream_key, shape, pieces, -0.22, 0.18) if pieces else 1.0
    result = jax.random.normal(stream_key, shape, jnp.float32) * spread * level
    return jnp.minimum(jnp.maximum(result, -bound), bound).astype(kind)


def setup_inputs(seed: int = 0) -> dict:
    streams_of = jax.random.split(jax.random.key(seed), 8)
    tokens = centred(streams_of[0], (TOKENS, D), 1.0, 6.0, ((0, 64),))
    w_query = draw_w_query(jax.random.fold_in(streams_of[7], 71), 0)
    w_key = draw_w_key(jax.random.fold_in(streams_of[7], 71), 0)
    w_value = centred(streams_of[3], (D, HEADS * HEAD_DIM), D ** -0.5, 0.078125, ((0, 64), (1, 8)))
    query_gain = draw_query_gain(jax.random.fold_in(streams_of[7], 71), 0)
    key_gain = draw_key_gain(jax.random.fold_in(streams_of[7], 71), 0)
    key_tiles = draw_key_tiles(jax.random.fold_in(streams_of[7], 71), 0)
    return dict(tokens=tokens, w_query=w_query, w_key=w_key, w_value=w_value, query_gain=query_gain, key_gain=key_gain, key_tiles=key_tiles)


def normalize(values, gain):
    mean_square = lax.optimization_barrier(jnp.mean(values * values, axis=1))
    return (values * lax.rsqrt(mean_square + 1e-06)[:, None] * gain[None, :]).astype(jnp.bfloat16)

def reference(tokens, w_query, w_key, w_value, query_gain, key_gain, key_tiles):
    query = jnp.dot(tokens, w_query, preferred_element_type=jnp.float32)
    key_full = jnp.dot(tokens, w_key, preferred_element_type=jnp.float32)
    value_cast = jnp.dot(tokens, w_value, preferred_element_type=jnp.float32).astype(jnp.bfloat16)
    query_normed = normalize(query, query_gain)
    key_normed = normalize(key_full, key_gain)
    tile_count = tokens.shape[0] // TILE
    queries = query_normed.reshape(tile_count, TILE, HEADS, HEAD_DIM)
    keys_tiled = key_normed.reshape(tile_count, TILE, HEADS, HEAD_DIM)
    values_tiled = value_cast.reshape(tile_count, TILE, HEADS, HEAD_DIM)

    def one_tile(inputs):
        query_block, entries = inputs
        usable = entries >= 0
        clipped = jnp.where(usable, entries, 0).astype(jnp.int32)
        chosen_keys = keys_tiled[clipped].astype(jnp.float32)
        chosen_values = values_tiled[clipped].astype(jnp.float32)
        scores = jnp.einsum('qhd,ckhd->hqck', query_block.astype(jnp.float32), chosen_keys, precision=lax.Precision.HIGHEST) * HEAD_DIM ** (-0.5)
        scores = jnp.where(usable[None, None, :, None], scores, -jnp.inf)
        highest = lax.optimization_barrier(jnp.max(scores, axis=(2, 3), keepdims=True))
        raised = jnp.exp(scores - highest)
        softmax_weights = (raised / lax.optimization_barrier(jnp.sum(raised, axis=(2, 3), keepdims=True))).astype(jnp.bfloat16)
        combined = jnp.einsum('hqck,ckhd->qhd', softmax_weights.astype(jnp.float32), chosen_values, precision=lax.Precision.HIGHEST)
        return combined.astype(jnp.bfloat16)
    attended = lax.map(one_tile, (queries, key_tiles))
    return attended.reshape(tokens.shape[0], HEADS * HEAD_DIM)
```

```python
import functools

import jax
import jax.numpy as jnp
from jax import lax
from jax.experimental import pallas as pl
from jax.experimental.pallas import tpu as pltpu
from jax.sharding import PartitionSpec as P

HEAD_DIM = 128
HEADS = 24
TILE = 128


def offsets_of(frames):
    near = [-1, 1, -2, 2]
    stride = 4
    while stride < frames // 2:
        near += [-stride, stride]
        stride *= 2
    return near


def scale_of(total, gain):
    return lax.rsqrt(total / (HEADS * HEAD_DIM) + 1e-06)[:, None] * gain[None, :]


def attend_kernel(heads_here, count, usable, query, *refs):
    pairs, out = refs[:count], refs[count]
    columns = heads_here * HEAD_DIM
    for head in range(heads_here):
        part = slice(head * HEAD_DIM, (head + 1) * HEAD_DIM)
        value_part = slice(columns + head * HEAD_DIM, columns + (head + 1) * HEAD_DIM)
        queries = query[:, part]
        scores = []
        for index in range(count):
            score = lax.dot_general(
                queries, pairs[index][:, part], (((1,), (1,)), ((), ())),
                preferred_element_type=jnp.float32,
            ) * HEAD_DIM ** (-0.5)
            scores.append(jnp.where(usable[index] > 0, score, -jnp.inf))
        highest = jnp.max(functools.reduce(jnp.maximum, scores), axis=1, keepdims=True)
        raised = [jnp.exp(score - highest) for score in scores]
        total = jnp.sum(functools.reduce(jnp.add, raised), axis=1, keepdims=True)
        combined = jnp.zeros((TILE, HEAD_DIM), jnp.float32)
        for index in range(count):
            combined += jnp.dot(
                raised[index].astype(jnp.bfloat16), pairs[index][:, value_part],
                preferred_element_type=jnp.float32,
            )
        out[:, part] = (combined / total).astype(out.dtype)


def attend(query, pairs, usable):
    count = len(pairs)
    rows, columns = query.shape
    heads_here = columns // HEAD_DIM
    vmem = pl.BlockSpec(memory_space=pltpu.VMEM)
    return pl.pallas_call(
        functools.partial(attend_kernel, heads_here, count),
        out_shape=jax.ShapeDtypeStruct((rows, columns), jnp.bfloat16),
        in_specs=[pl.BlockSpec(memory_space=pltpu.SMEM)] + [vmem] * (count + 1),
        out_specs=vmem,
        cost_estimate=pl.CostEstimate(
            flops=4 * rows * rows * columns * count,
            bytes_accessed=2 * rows * columns * (2 * count + 2),
            transcendentals=rows * rows * heads_here * count,
        ),
    )(usable, query, *pairs)


def on_device(tokens, w_query, w_key, w_value, query_gain, key_gain, key_tiles):
    frames = lax.axis_size("frame")
    position = lax.axis_index("frame")
    columns = w_query.shape[1]

    panel = jnp.concatenate([w_key, w_value, w_query], axis=1)
    gathered = lax.all_gather(panel, "frame", axis=0, tiled=True)
    projected = jnp.dot(tokens, gathered, preferred_element_type=jnp.float32)
    key_full = projected[:, :columns]
    value_full = projected[:, columns : 2 * columns]
    query = projected[:, 2 * columns :]
    totals = lax.psum(
        jnp.stack([jnp.sum(key_full * key_full, axis=1), jnp.sum(query * query, axis=1)]), "head"
    )
    key_normed = (key_full * scale_of(totals[0], key_gain)).astype(jnp.bfloat16)
    paired = jnp.concatenate([key_normed, value_full.astype(jnp.bfloat16)], axis=1)

    own_row = lax.dynamic_slice_in_dim(key_tiles, position, 1, 0)[0]
    pairs, tiles = [paired], [position]
    half = frames // 2
    pairs.append(lax.ppermute(paired, "frame", [(s, (s + half) % frames) for s in range(frames)]))
    tiles.append((position + half) % frames)
    for offset in reversed(offsets_of(frames)):
        route = [(s, s - offset) for s in range(frames) if 0 <= s - offset < frames]
        pairs.append(lax.ppermute(paired, "frame", route))
        tiles.append(position + offset)
    tiles = jnp.stack(tiles)
    named = jnp.any(own_row[None, :] == tiles[:, None], axis=1)
    usable = (named & (tiles >= 0) & (tiles < frames)).astype(jnp.int32)

    query_normed = (query * scale_of(totals[1], query_gain)).astype(jnp.bfloat16)
    return attend(query_normed, pairs, usable)


def solution(mesh):
    return jax.shard_map(
        on_device,
        mesh=mesh,
        in_specs=(
            P("frame", None),
            P("frame", "head"),
            P("frame", "head"),
            P("frame", "head"),
            P("head"),
            P("head"),
            P(),
        ),
        out_specs=P("frame", "head"),
        check_vma=False,
    )
```

```python
import functools

import jax
import jax.numpy as jnp
from jax import lax
from jax.experimental import pallas as pl
from jax.experimental.pallas import tpu as pltpu
from jax.sharding import Mesh, PartitionSpec as P

HEAD_DIM = 128
HEADS = 24
TILE = 128


def swaps_of(frames):
    swaps = []
    stride = 1
    while stride <= frames // 2:
        swaps.append((stride, [tile ^ stride for tile in range(frames)]))
        if stride < frames // 2:
            other = [tile + stride if tile & stride else tile - stride for tile in range(frames)]
            swaps.append((stride, [mate if 0 <= mate < frames else -2 for mate in other]))
        stride *= 2
    first, second = swaps[0::2], swaps[1::2]
    far = lambda swap: -min(swap[0], 12)
    ordered = sorted(first + second, key=far)
    return [mates for _, mates in ordered]


def swapped(value, axis, distance):
    count = lax.axis_size(axis)
    return lax.ppermute(value, axis, [(index, index ^ distance) for index in range(count)])


def summed_over(value, axis):
    distance = 1
    while distance < lax.axis_size(axis):
        value = value + swapped(value, axis, distance)
        distance *= 2
    return value


def scale_of(total, gain):
    return lax.rsqrt(total / (HEADS * HEAD_DIM) + 1e-06)[:, None] * gain[None, :]


def attend_kernel(heads_here, count, usable, query, *refs):
    pairs, out = refs[:count], refs[count]
    columns = heads_here * HEAD_DIM
    for head in range(heads_here):
        part = slice(head * HEAD_DIM, (head + 1) * HEAD_DIM)
        value_part = slice(columns + head * HEAD_DIM, columns + (head + 1) * HEAD_DIM)
        queries = query[:, part]
        scores = []
        for index in range(count):
            score = lax.dot_general(
                queries, pairs[index][:, part], (((1,), (1,)), ((), ())),
                preferred_element_type=jnp.float32,
            ) * HEAD_DIM ** (-0.5)
            scores.append(jnp.where(usable[index] > 0, score, -jnp.inf))
        highest = jnp.max(functools.reduce(jnp.maximum, scores), axis=1, keepdims=True)
        raised = [jnp.exp(score - highest) for score in scores]
        total = jnp.sum(functools.reduce(jnp.add, raised), axis=1, keepdims=True)
        combined = jnp.zeros((TILE, HEAD_DIM), jnp.float32)
        for index in range(count):
            combined += jnp.dot(
                raised[index].astype(jnp.bfloat16), pairs[index][:, value_part],
                preferred_element_type=jnp.float32,
            )
        out[:, part] = (combined / total).astype(out.dtype)


def attend(query, pairs, usable):
    count = len(pairs)
    rows, columns = query.shape
    heads_here = columns // HEAD_DIM
    vmem = pl.BlockSpec(memory_space=pltpu.VMEM)
    return pl.pallas_call(
        functools.partial(attend_kernel, heads_here, count),
        out_shape=jax.ShapeDtypeStruct((rows, columns), jnp.bfloat16),
        in_specs=[pl.BlockSpec(memory_space=pltpu.SMEM)] + [vmem] * (count + 1),
        out_specs=vmem,
        cost_estimate=pl.CostEstimate(
            flops=4 * rows * rows * columns * count,
            bytes_accessed=2 * rows * columns * (2 * count + 2),
            transcendentals=rows * rows * heads_here * count,
        ),
    )(usable, query, *pairs)


FRAME = ("x", "z", "core")


def on_device(tokens, w_query, w_key, w_value, query_gain, key_gain, key_tiles):
    frames = lax.axis_size(FRAME)
    position = lax.axis_index(FRAME)
    columns = w_query.shape[1]
    rows, width = tokens.shape
    parts = lax.axis_size("x")
    here = lax.axis_index("x")
    depth = width // parts

    panel = jnp.concatenate([w_key, w_value, w_query], axis=1)
    gathered = lax.all_gather(panel, ("z", "core"), axis=0, tiled=True)

    def columns_of(part):
        return lax.dynamic_slice_in_dim(tokens, part * depth, depth, 1)

    others = range(1, parts)
    received = [swapped(columns_of(here ^ other), "x", other) for other in others]
    foreign = jnp.dot(
        jnp.concatenate(received, axis=0), gathered, preferred_element_type=jnp.float32
    ).astype(jnp.bfloat16)
    own = jnp.dot(columns_of(here), gathered, preferred_element_type=jnp.float32)
    projected = own
    for other in others:
        part = foreign[(other - 1) * rows : other * rows]
        projected = projected + swapped(part, "x", other).astype(jnp.float32)

    key_full = projected[:, :columns]
    value_full = projected[:, columns : 2 * columns]
    query = projected[:, 2 * columns :]
    totals = summed_over(
        jnp.stack([jnp.sum(key_full * key_full, axis=1), jnp.sum(query * query, axis=1)]), "head"
    )
    key_normed = (key_full * scale_of(totals[0], key_gain)).astype(jnp.bfloat16)
    paired = jnp.concatenate([key_normed, value_full.astype(jnp.bfloat16)], axis=1)

    swaps = swaps_of(frames)
    met = jnp.asarray([list(tiles) for tiles in zip(range(frames), *swaps)], jnp.int32)
    own_row = lax.dynamic_slice_in_dim(key_tiles, position, 1, 0)
    met_here = lax.dynamic_slice_in_dim(met, position, 1, 0)
    usable = jnp.any(own_row[0, None, :] == met_here[0, :, None], axis=1).astype(jnp.int32)
    pairs = [paired]
    for mates in swaps:
        route = [(tile, mate) for tile, mate in enumerate(mates) if mate >= 0]
        pairs.append(lax.ppermute(paired, FRAME, route))

    query_normed = (query * scale_of(totals[1], query_gain)).astype(jnp.bfloat16)
    return attend(query_normed, pairs, usable)


def solution(mesh):
    shape = (4, mesh.shape["frame"] // 8, 2, mesh.shape["head"])
    split = Mesh(mesh.devices.reshape(shape), FRAME + ("head",))
    return jax.shard_map(
        on_device,
        mesh=split,
        in_specs=(
            P(FRAME, None),
            P(FRAME, "head"),
            P(FRAME, "head"),
            P(FRAME, "head"),
            P("head"),
            P("head"),
            P(),
        ),
        out_specs=P(FRAME, "head"),
        check_vma=False,
    )
```

```python
import functools

import jax
import jax.numpy as jnp
from jax import lax
from jax.experimental import pallas as pl
from jax.experimental.pallas import tpu as pltpu
from jax.sharding import Mesh, PartitionSpec as P

HEAD_DIM = 128
HEADS = 24
TILE = 128
FRAME = ("x", "z", "core")


def mates_of(frames, stride):
    first = [tile ^ stride for tile in range(frames)]
    second = [tile + stride if tile & stride else tile - stride for tile in range(frames)]
    return first, [mate if 0 <= mate < frames else -2 for mate in second]


def pass_along(value, mates):
    route = [(tile, mate) for tile, mate in enumerate(mates) if mate >= 0]
    return lax.ppermute(value, FRAME, route)


def swapped(value, axis, distance):
    count = lax.axis_size(axis)
    return lax.ppermute(value, axis, [(index, index ^ distance) for index in range(count)])


def collect(paired, frames):
    pairs, tiles = [paired], [list(range(frames))]
    first, second = mates_of(frames, 4)
    from_first, from_second = pass_along(paired, first), pass_along(paired, second)
    pairs += [from_first, from_second]
    tiles += [first, second]
    for mates in mates_of(frames, 16):
        pairs.append(pass_along(paired, mates))
        tiles.append(mates)
    paired, from_first, from_second = lax.optimization_barrier((paired, from_first, from_second))
    for stride in (1, 2, 32):
        for mates in mates_of(frames, stride)[: 1 if stride == 32 else 2]:
            pairs.append(pass_along(paired, mates))
            tiles.append(mates)
    for value, route, held in ((from_first, second, first), (from_second, first, second)):
        pairs.append(pass_along(value, route))
        tiles.append([held[mate] if mate >= 0 else -2 for mate in route])
    return pairs, tiles


def scale_of(total, gain):
    return lax.rsqrt(total / (HEADS * HEAD_DIM) + 1e-06)[:, None] * gain[None, :]


def attend_kernel(heads_here, count, usable, query, *refs):
    pairs, out = refs[:count], refs[count]
    columns = heads_here * HEAD_DIM
    for head in range(heads_here):
        part = slice(head * HEAD_DIM, (head + 1) * HEAD_DIM)
        value_part = slice(columns + head * HEAD_DIM, columns + (head + 1) * HEAD_DIM)
        queries = query[:, part]
        scores = []
        for index in range(count):
            score = lax.dot_general(
                queries, pairs[index][:, part], (((1,), (1,)), ((), ())),
                preferred_element_type=jnp.float32,
            ) * HEAD_DIM ** (-0.5)
            scores.append(jnp.where(usable[index] > 0, score, -jnp.inf))
        highest = jnp.max(functools.reduce(jnp.maximum, scores), axis=1, keepdims=True)
        raised = [jnp.exp(score - highest) for score in scores]
        total = jnp.sum(functools.reduce(jnp.add, raised), axis=1, keepdims=True)
        combined = jnp.zeros((TILE, HEAD_DIM), jnp.float32)
        for index in range(count):
            combined += jnp.dot(
                raised[index].astype(jnp.bfloat16), pairs[index][:, value_part],
                preferred_element_type=jnp.float32,
            )
        out[:, part] = (combined / total).astype(out.dtype)


def attend(query, pairs, usable):
    count = len(pairs)
    rows, columns = query.shape
    heads_here = columns // HEAD_DIM
    vmem = pl.BlockSpec(memory_space=pltpu.VMEM)
    return pl.pallas_call(
        functools.partial(attend_kernel, heads_here, count),
        out_shape=jax.ShapeDtypeStruct((rows, columns), jnp.bfloat16),
        in_specs=[pl.BlockSpec(memory_space=pltpu.SMEM)] + [vmem] * (count + 1),
        out_specs=vmem,
        cost_estimate=pl.CostEstimate(
            flops=4 * rows * rows * columns * count,
            bytes_accessed=2 * rows * columns * (2 * count + 2),
            transcendentals=rows * rows * heads_here * count,
        ),
    )(usable, query, *pairs)


def on_device(tokens, w_query, w_key, w_value, query_gain, key_gain, key_tiles):
    frames = lax.axis_size(FRAME)
    position = lax.axis_index(FRAME)
    columns = w_query.shape[1]
    rows, width = tokens.shape
    parts = lax.axis_size("x")
    here = lax.axis_index("x")
    depth = width // parts

    panel = jnp.concatenate([w_key, w_value, w_query], axis=1)
    gathered = lax.all_gather(panel, ("z", "core"), axis=0, tiled=True)

    def columns_of(part):
        return lax.dynamic_slice_in_dim(tokens, part * depth, depth, 1)

    received = [swapped(columns_of(here ^ other), "x", other) for other in (2, 1, 3)]
    foreign = jnp.dot(
        jnp.concatenate(received, axis=0), gathered, preferred_element_type=jnp.float32
    ).astype(jnp.bfloat16)
    opposite, left, right = (foreign[index * rows : (index + 1) * rows] for index in range(3))
    own = jnp.dot(columns_of(here), gathered, preferred_element_type=jnp.float32)

    cut = 640
    to_left = jnp.concatenate([opposite[:, :cut], left[:, :cut]], axis=1)
    to_right = jnp.concatenate([opposite[:, cut:], right[:, cut:]], axis=1)
    from_left, from_right = swapped(to_left, "x", 1), swapped(to_right, "x", 3)

    def plus(partial, passing):
        return (partial.astype(jnp.float32) + passing.astype(jnp.float32)).astype(jnp.bfloat16)

    late_right = swapped(plus(right[:, :cut], from_left[:, :cut]), "x", 3)
    late_left = swapped(plus(left[:, cut:], from_right[:, : columns * 3 - cut]), "x", 1)
    projected = (
        own
        + jnp.concatenate([from_left[:, cut:], from_right[:, columns * 3 - cut :]], axis=1).astype(jnp.float32)
        + jnp.concatenate([late_right, late_left], axis=1).astype(jnp.float32)
    )

    key_full = projected[:, :columns]
    value_full = projected[:, columns : 2 * columns]
    query = projected[:, 2 * columns :]
    totals = lax.psum(
        jnp.stack([jnp.sum(key_full * key_full, axis=1), jnp.sum(query * query, axis=1)]), "head"
    )
    key_normed = (key_full * scale_of(totals[0], key_gain)).astype(jnp.bfloat16)
    paired = jnp.concatenate([key_normed, value_full.astype(jnp.bfloat16)], axis=1)

    pairs, tiles = collect(paired, frames)
    met = jnp.asarray([list(each) for each in zip(*tiles)], jnp.int32)
    own_row = lax.dynamic_slice_in_dim(key_tiles, position, 1, 0)
    met_here = lax.dynamic_slice_in_dim(met, position, 1, 0)
    usable = jnp.any(own_row[0, None, :] == met_here[0, :, None], axis=1).astype(jnp.int32)

    query_normed = (query * scale_of(totals[1], query_gain)).astype(jnp.bfloat16)
    return attend(query_normed, pairs, usable)


def solution(mesh):
    shape = (4, mesh.shape["frame"] // 8, 2, mesh.shape["head"])
    split = Mesh(mesh.devices.reshape(shape), FRAME + ("head",))
    return jax.shard_map(
        on_device,
        mesh=split,
        in_specs=(
            P(FRAME, None),
            P(FRAME, "head"),
            P(FRAME, "head"),
            P(FRAME, "head"),
            P("head"),
            P("head"),
            P(),
        ),
        out_specs=P(FRAME, "head"),
        check_vma=False,
    )
```

```python
import functools

import jax
import jax.numpy as jnp
from jax import lax
from jax.experimental import pallas as pl
from jax.experimental.pallas import tpu as pltpu
from jax.sharding import Mesh, PartitionSpec as P

HEAD_DIM = 128
HEADS = 24
TILE = 128
FRAME = ("x", "z", "core")


def swapped(value, axis, distance):
    count = lax.axis_size(axis)
    return lax.ppermute(value, axis, [(index, index ^ distance) for index in range(count)])


def chip_swap(frames, apart):
    starts = range(0, frames - 2 * apart, 2)
    there = [(tile, tile + 2 * apart + 1) for tile in starts]
    return there + [(back, tile) for tile, back in there]


def chip_relay(frames, apart):
    first = [(tile + 2 * apart, tile) for tile in range(0, frames - 2 * apart, 2)]
    second = [(tile, tile + 2 * apart) for tile in range(1, frames - 2 * apart, 2)]
    return first + second


def collect(paired, frames):
    def send(value, route):
        return lax.ppermute(value, FRAME, route)

    def traded(value):
        return send(value, [(tile, tile ^ 1) for tile in range(frames)])

    mate = traded(paired)
    far = send(paired, [(tile, (tile + frames // 2) % frames) for tile in range(frames)])
    both = jnp.concatenate([paired, mate], axis=0)
    two = send(both, chip_swap(frames, 2))
    one = send(both, chip_swap(frames, 1))
    eight = send(both, chip_swap(frames, 8))
    four = send(two, chip_relay(frames, 2))
    one, far = lax.optimization_barrier((one, far))
    crossed = traded(jnp.concatenate([one, two[:TILE], eight[:TILE], four[:TILE]], axis=0))
    return [
        (paired, 0), (mate, 0), (far, 0), (one, 1), (two, 1), (four, 1), (eight, 1),
        (crossed, 0), (crossed, 1), (crossed, 2), (crossed, 3), (crossed, 4),
    ]


def tiles_met(frames):
    table = []
    for tile in range(frames):
        chip, core = divmod(tile, 2)
        side = 1 - 2 * core

        def at(apart, parity):
            return 2 * (chip + apart) + parity if 0 <= chip + apart < frames // 2 else -2

        direct = [at(side * apart, core) for apart in (1, 2, 4, 8)]
        crossed = [at(-side, core), at(-side, 1 - core)]
        crossed += [at(-side * apart, core) for apart in (2, 8, 4)]
        table.append([tile, tile ^ 1, (tile + frames // 2) % frames] + direct + crossed)
    return table


def scale_of(total, gain):
    return lax.rsqrt(total / (HEADS * HEAD_DIM) + 1e-06)[:, None] * gain[None, :]


def attend_kernel(heads_here, places, usable, query, *refs):
    out = refs[-1]
    columns = heads_here * HEAD_DIM
    for head in range(heads_here):
        part = slice(head * HEAD_DIM, (head + 1) * HEAD_DIM)
        value_part = slice(columns + head * HEAD_DIM, columns + (head + 1) * HEAD_DIM)
        queries = query[:, part]
        scores = []
        for index, (block, row) in enumerate(places):
            score = lax.dot_general(
                queries, refs[block][row * TILE : (row + 1) * TILE, part], (((1,), (1,)), ((), ())),
                preferred_element_type=jnp.float32,
            ) * HEAD_DIM ** (-0.5)
            scores.append(jnp.where(usable[index] > 0, score, -jnp.inf))
        highest = jnp.max(functools.reduce(jnp.maximum, scores), axis=1, keepdims=True)
        raised = [jnp.exp(score - highest) for score in scores]
        total = jnp.sum(functools.reduce(jnp.add, raised), axis=1, keepdims=True)
        combined = jnp.zeros((TILE, HEAD_DIM), jnp.float32)
        for index, (block, row) in enumerate(places):
            combined += jnp.dot(
                raised[index].astype(jnp.bfloat16),
                refs[block][row * TILE : (row + 1) * TILE, value_part],
                preferred_element_type=jnp.float32,
            )
        out[:, part] = (combined / total).astype(out.dtype)


def attend(query, blocks, usable):
    arrays, places = [], []
    for array, row in blocks:
        known = [index for index, other in enumerate(arrays) if other is array]
        if not known:
            arrays.append(array)
        places.append((known[0] if known else len(arrays) - 1, row))
    rows, columns = query.shape
    heads_here = columns // HEAD_DIM
    count = len(blocks)
    vmem = pl.BlockSpec(memory_space=pltpu.VMEM)
    return pl.pallas_call(
        functools.partial(attend_kernel, heads_here, places),
        out_shape=jax.ShapeDtypeStruct((rows, columns), jnp.bfloat16),
        in_specs=[pl.BlockSpec(memory_space=pltpu.SMEM)] + [vmem] * (len(arrays) + 1),
        out_specs=vmem,
        cost_estimate=pl.CostEstimate(
            flops=4 * rows * rows * columns * count,
            bytes_accessed=2 * rows * columns * (2 * count + 2),
            transcendentals=rows * rows * heads_here * count,
        ),
    )(usable, query, *arrays)


def on_device(tokens, w_query, w_key, w_value, query_gain, key_gain, key_tiles):
    frames = lax.axis_size(FRAME)
    position = lax.axis_index(FRAME)
    columns = w_query.shape[1]
    rows, width = tokens.shape
    parts = lax.axis_size("x")
    here = lax.axis_index("x")
    depth = width // parts

    panel = jnp.concatenate([w_key, w_value, w_query], axis=1)
    gathered = lax.all_gather(panel, ("z", "core"), axis=0, tiled=True)

    def columns_of(part):
        return lax.dynamic_slice_in_dim(tokens, part * depth, depth, 1)

    held = [columns_of(here)] + [swapped(columns_of(here ^ other), "x", other) for other in range(1, parts)]
    held = jnp.stack(held)
    ordered = [lax.dynamic_index_in_dim(held, here ^ part, 0, keepdims=False) for part in range(parts)]
    partial = jnp.dot(
        jnp.concatenate(ordered, axis=0), gathered, preferred_element_type=jnp.float32
    ).astype(jnp.bfloat16)
    partial = lax.all_to_all(partial.reshape(parts, rows, -1), "x", 0, 0)
    projected = jnp.sum(partial.astype(jnp.float32), axis=0)

    key_full = projected[:, :columns]
    value_full = projected[:, columns : 2 * columns]
    query = projected[:, 2 * columns :]
    squares = jnp.stack([jnp.sum(key_full * key_full, axis=1), jnp.sum(query * query, axis=1)])
    count = lax.axis_size("head")
    squares = lax.all_to_all(jnp.broadcast_to(squares[None], (count, 2, rows)), "head", 0, 0)
    totals = jnp.sum(squares, axis=0)
    key_normed = (key_full * scale_of(totals[0], key_gain)).astype(jnp.bfloat16)
    paired = jnp.concatenate([key_normed, value_full.astype(jnp.bfloat16)], axis=1)

    blocks = collect(paired, frames)
    met = jnp.asarray(tiles_met(frames), jnp.int32)
    own_row = lax.dynamic_slice_in_dim(key_tiles, position, 1, 0)
    met_here = lax.dynamic_slice_in_dim(met, position, 1, 0)
    usable = jnp.any(own_row[0, None, :] == met_here[0, :, None], axis=1).astype(jnp.int32)

    query_normed = (query * scale_of(totals[1], query_gain)).astype(jnp.bfloat16)
    return attend(query_normed, blocks, usable)


def solution(mesh):
    shape = (4, mesh.shape["frame"] // 8, 2, mesh.shape["head"])
    split = Mesh(mesh.devices.reshape(shape), FRAME + ("head",))
    return jax.shard_map(
        on_device,
        mesh=split,
        in_specs=(
            P(FRAME, None),
            P(FRAME, "head"),
            P(FRAME, "head"),
            P(FRAME, "head"),
            P("head"),
            P("head"),
            P(),
        ),
        out_specs=P(FRAME, "head"),
        check_vma=False,
    )
```

```python
import functools

import jax
import jax.numpy as jnp
from jax import lax
from jax.experimental import pallas as pl
from jax.experimental.pallas import tpu as pltpu
from jax.sharding import Mesh, PartitionSpec as P

HEAD_DIM = 128
HEADS = 24
TILE = 128
FRAME = ("x", "z", "core")


def swapped(value, axis, distance):
    count = lax.axis_size(axis)
    return lax.ppermute(value, axis, [(index, index ^ distance) for index in range(count)])


def chip_swap(frames, apart):
    starts = range(0, frames - 2 * apart, 2)
    there = [(tile, tile + 2 * apart + 1) for tile in starts]
    return there + [(back, tile) for tile, back in there]


def chip_relay(frames, apart):
    first = [(tile + 2 * apart, tile) for tile in range(0, frames - 2 * apart, 2)]
    second = [(tile, tile + 2 * apart) for tile in range(1, frames - 2 * apart, 2)]
    return first + second


def core_trade(value):
    return lax.ppermute(value, "core", [(0, 1), (1, 0)])


def collect(paired, query_square, frames):
    def send(value, route):
        return lax.ppermute(value, FRAME, route)

    mate = core_trade(paired)
    both = jnp.concatenate([paired, mate], axis=0)
    far = send(paired, [(tile, (tile + frames // 2) % frames) for tile in range(frames)])
    two = send(both, chip_swap(frames, 2))
    both, query_square = lax.optimization_barrier((both, query_square))
    query_total = lax.psum(query_square, "head")
    one = send(both, chip_swap(frames, 1))
    eight = send(both, chip_swap(frames, 8))
    two, far = lax.optimization_barrier((two, far))
    four = send(two, chip_relay(frames, 2))
    one, query_total = lax.optimization_barrier((one, query_total))
    crossed = core_trade(jnp.concatenate([one, two[:TILE], eight[:TILE], four[:TILE]], axis=0))
    return [
        (paired, 0), (mate, 0), (far, 0), (one, 1), (two, 1), (four, 1), (eight, 1),
        (crossed, 0), (crossed, 1), (crossed, 2), (crossed, 3), (crossed, 4),
    ], query_total


def tiles_met(frames):
    table = []
    for tile in range(frames):
        chip, core = divmod(tile, 2)
        side = 1 - 2 * core

        def at(apart, parity):
            return 2 * (chip + apart) + parity if 0 <= chip + apart < frames // 2 else -2

        direct = [at(side * apart, core) for apart in (1, 2, 4, 8)]
        crossed = [at(-side, core), at(-side, 1 - core)]
        crossed += [at(-side * apart, core) for apart in (2, 8, 4)]
        table.append([tile, tile ^ 1, (tile + frames // 2) % frames] + direct + crossed)
    return table


def attend_kernel(heads_here, places, usable, query, query_total, query_gain, *refs):
    out = refs[-1]
    query_scale = lax.rsqrt(query_total[...] / (HEADS * HEAD_DIM) + 1e-06)
    columns = heads_here * HEAD_DIM
    for head in range(heads_here):
        part = slice(head * HEAD_DIM, (head + 1) * HEAD_DIM)
        value_part = slice(columns + head * HEAD_DIM, columns + (head + 1) * HEAD_DIM)
        queries = (query[:, part] * query_scale * query_gain[:, part]).astype(jnp.bfloat16)
        scores = []
        for index, (block, row) in enumerate(places):
            score = lax.dot_general(
                queries, refs[block][row * TILE : (row + 1) * TILE, part], (((1,), (1,)), ((), ())),
                preferred_element_type=jnp.float32,
            ) * HEAD_DIM ** (-0.5)
            scores.append(jnp.where(usable[index] > 0, score, -jnp.inf))
        highest = jnp.max(functools.reduce(jnp.maximum, scores), axis=1, keepdims=True)
        raised = [jnp.exp(score - highest) for score in scores]
        total = jnp.sum(functools.reduce(jnp.add, raised), axis=1, keepdims=True)
        combined = jnp.zeros((TILE, HEAD_DIM), jnp.float32)
        for index, (block, row) in enumerate(places):
            combined += jnp.dot(
                raised[index].astype(jnp.bfloat16),
                refs[block][row * TILE : (row + 1) * TILE, value_part],
                preferred_element_type=jnp.float32,
            )
        out[:, part] = (combined / total).astype(out.dtype)


def attend(query, query_total, query_gain, blocks, usable):
    arrays, places = [], []
    for array, row in blocks:
        known = [index for index, other in enumerate(arrays) if other is array]
        if not known:
            arrays.append(array)
        places.append((known[0] if known else len(arrays) - 1, row))
    rows, columns = query.shape
    heads_here = columns // HEAD_DIM
    count = len(blocks)
    vmem = pl.BlockSpec(memory_space=pltpu.VMEM)
    return pl.pallas_call(
        functools.partial(attend_kernel, heads_here, places),
        out_shape=jax.ShapeDtypeStruct((rows, columns), jnp.bfloat16),
        in_specs=[pl.BlockSpec(memory_space=pltpu.SMEM)] + [vmem] * (len(arrays) + 3),
        out_specs=vmem,
        cost_estimate=pl.CostEstimate(
            flops=4 * rows * rows * columns * count,
            bytes_accessed=2 * rows * columns * (2 * count + 2),
            transcendentals=rows * rows * heads_here * count,
        ),
    )(usable, query, query_total, query_gain[None, :], *arrays)


def on_device(tokens, w_query, w_key, w_value, query_gain, key_gain, key_tiles):
    frames = lax.axis_size(FRAME)
    position = lax.axis_index(FRAME)
    columns = w_query.shape[1]
    rows, width = tokens.shape
    parts = lax.axis_size("x")
    here = lax.axis_index("x")
    depth = width // parts

    def columns_of(part):
        return lax.dynamic_slice_in_dim(tokens, part * depth, depth, 1)

    held = [columns_of(here)] + [swapped(columns_of(here ^ other), "x", other) for other in range(1, parts)]
    held = jnp.stack(held)
    ordered = [lax.dynamic_index_in_dim(held, here ^ part, 0, keepdims=False) for part in range(parts)]
    held = jnp.concatenate(ordered, axis=0)

    def partial_of(panel):
        return jnp.dot(held, panel, preferred_element_type=jnp.float32).astype(jnp.bfloat16)

    panel = jnp.concatenate([w_key, w_value, w_query], axis=1)
    panel = lax.all_gather(panel, ("z", "core"), axis=0, tiled=True)
    pair_parts = partial_of(panel[:, : 2 * columns]).reshape(parts, rows, 2 * columns)
    pair = jnp.sum(lax.all_to_all(pair_parts, "x", 0, 0).astype(jnp.float32), axis=0)
    key_full, value_full = pair[:, :columns], pair[:, columns:]

    squares = jnp.sum(key_full * key_full, axis=1)
    query_parts = partial_of(panel[:, 2 * columns :])
    squares, query_parts = lax.optimization_barrier((squares, query_parts))
    count = lax.axis_size("head")
    squares = lax.all_to_all(jnp.broadcast_to(squares[None, None], (count, 1, rows)), "head", 0, 0)
    key_scale = lax.rsqrt(jnp.sum(squares, axis=(0, 1)) / (HEADS * HEAD_DIM) + 1e-06)
    key_normed = (key_full * key_scale[:, None] * key_gain[None, :]).astype(jnp.bfloat16)
    paired = jnp.concatenate([key_normed, value_full.astype(jnp.bfloat16)], axis=1)

    query = lax.psum_scatter(query_parts, "x", scatter_dimension=0, tiled=True)
    query = query.astype(jnp.float32)
    query_square = jnp.broadcast_to(jnp.sum(query * query, axis=1, keepdims=True), (rows, HEAD_DIM))
    blocks, query_total = collect(paired, query_square, frames)
    met = jnp.asarray(tiles_met(frames), jnp.int32)
    own_row = lax.dynamic_slice_in_dim(key_tiles, position, 1, 0)
    met_here = lax.dynamic_slice_in_dim(met, position, 1, 0)
    usable = jnp.any(own_row[0, None, :] == met_here[0, :, None], axis=1).astype(jnp.int32)
    return attend(query, query_total, query_gain, blocks, usable)


def solution(mesh):
    shape = (4, mesh.shape["frame"] // 8, 2, mesh.shape["head"])
    split = Mesh(mesh.devices.reshape(shape), FRAME + ("head",))
    return jax.shard_map(
        on_device,
        mesh=split,
        in_specs=(
            P(FRAME, None),
            P(FRAME, "head"),
            P(FRAME, "head"),
            P(FRAME, "head"),
            P("head"),
            P("head"),
            P(),
        ),
        out_specs=P(FRAME, "head"),
        check_vma=False,
    )
```

```python
import functools

import jax
import jax.numpy as jnp
from jax import lax
from jax.experimental import pallas as pl
from jax.experimental.pallas import tpu as pltpu
from jax.sharding import Mesh, PartitionSpec as P

HEAD_DIM = 128
HEADS = 24
TILE = 128
FRAME = ("x", "z", "core")


def swapped(value, axis, distance):
    count = lax.axis_size(axis)
    return lax.ppermute(value, axis, [(index, index ^ distance) for index in range(count)])


def chip_swap(frames, apart):
    starts = range(0, frames - 2 * apart, 2)
    there = [(tile, tile + 2 * apart + 1) for tile in starts]
    return there + [(back, tile) for tile, back in there]


def chip_relay(frames, apart):
    first = [(tile + 2 * apart, tile) for tile in range(0, frames - 2 * apart, 2)]
    second = [(tile, tile + 2 * apart) for tile in range(1, frames - 2 * apart, 2)]
    return first + second


def core_trade(value):
    return lax.ppermute(value, "core", [(0, 1), (1, 0)])


def summed_over(value, axis):
    count = lax.axis_size(axis)
    everyone = lax.all_to_all(jnp.broadcast_to(value[None], (count,) + value.shape), axis, 0, 0)
    return jnp.sum(everyone, axis=0)


def scale_of(total):
    return lax.rsqrt(total / (HEADS * HEAD_DIM) + 1e-06)


def collect(paired, query, frames):
    def send(value, route):
        return lax.ppermute(value, FRAME, route)

    mate = core_trade(paired)
    both = jnp.concatenate([paired, mate], axis=0)
    far = send(paired, [(tile, (tile + frames // 2) % frames) for tile in range(frames)])
    two = send(both, chip_swap(frames, 2))
    one = send(both, chip_swap(frames, 1))
    eight = send(both, chip_swap(frames, 8))
    square = jnp.sum(query * query, axis=1)[None]
    two, square = lax.optimization_barrier((two, square))
    four = send(two, chip_relay(frames, 2))
    query_scale = scale_of(summed_over(square, "head"))
    one, far, query_scale = lax.optimization_barrier((one, far, query_scale))
    crossed = core_trade(jnp.concatenate([one, two[:TILE], eight[:TILE], four[:TILE]], axis=0))
    return [
        (paired, 0), (mate, 0), (far, 0), (one, 1), (two, 1), (four, 1), (eight, 1),
        (crossed, 0), (crossed, 1), (crossed, 2), (crossed, 3), (crossed, 4),
    ], query_scale[0]


def tiles_met(frames):
    table = []
    for tile in range(frames):
        chip, core = divmod(tile, 2)
        side = 1 - 2 * core

        def at(apart, parity):
            return 2 * (chip + apart) + parity if 0 <= chip + apart < frames // 2 else -2

        direct = [at(side * apart, core) for apart in (1, 2, 4, 8)]
        crossed = [at(-side, core), at(-side, 1 - core)]
        crossed += [at(-side * apart, core) for apart in (2, 8, 4)]
        table.append([tile, tile ^ 1, (tile + frames // 2) % frames] + direct + crossed)
    return table


def attend_kernel(heads_here, places, usable, query, query_scale, query_gain, *refs):
    out = refs[-1]
    columns = heads_here * HEAD_DIM
    for head in range(heads_here):
        part = slice(head * HEAD_DIM, (head + 1) * HEAD_DIM)
        value_part = slice(columns + head * HEAD_DIM, columns + (head + 1) * HEAD_DIM)
        queries = (query[:, part] * query_scale[...] * query_gain[:, part]).astype(jnp.bfloat16)
        scores = []
        for index, (block, row) in enumerate(places):
            score = lax.dot_general(
                queries, refs[block][row * TILE : (row + 1) * TILE, part], (((1,), (1,)), ((), ())),
                preferred_element_type=jnp.float32,
            ) * HEAD_DIM ** (-0.5)
            scores.append(jnp.where(usable[index] > 0, score, -jnp.inf))
        highest = jnp.max(functools.reduce(jnp.maximum, scores), axis=1, keepdims=True)
        raised = [jnp.exp(score - highest) for score in scores]
        total = jnp.sum(functools.reduce(jnp.add, raised), axis=1, keepdims=True)
        combined = jnp.zeros((TILE, HEAD_DIM), jnp.float32)
        for index, (block, row) in enumerate(places):
            combined += jnp.dot(
                raised[index].astype(jnp.bfloat16),
                refs[block][row * TILE : (row + 1) * TILE, value_part],
                preferred_element_type=jnp.float32,
            )
        out[:, part] = (combined / total).astype(out.dtype)


def attend(query, query_scale, query_gain, blocks, usable):
    arrays, places = [], []
    for array, row in blocks:
        known = [index for index, other in enumerate(arrays) if other is array]
        if not known:
            arrays.append(array)
        places.append((known[0] if known else len(arrays) - 1, row))
    rows, columns = query.shape
    heads_here = columns // HEAD_DIM
    count = len(blocks)
    vmem = pl.BlockSpec(memory_space=pltpu.VMEM)
    return pl.pallas_call(
        functools.partial(attend_kernel, heads_here, places),
        out_shape=jax.ShapeDtypeStruct((rows, columns), jnp.bfloat16),
        in_specs=[pl.BlockSpec(memory_space=pltpu.SMEM)] + [vmem] * (len(arrays) + 3),
        out_specs=vmem,
        cost_estimate=pl.CostEstimate(
            flops=4 * rows * rows * columns * count,
            bytes_accessed=2 * rows * columns * (2 * count + 2),
            transcendentals=rows * rows * heads_here * count,
        ),
    )(usable, query, query_scale, query_gain[None, :], *arrays)


def on_device(tokens, w_query, w_key, w_value, query_gain, key_gain, key_tiles):
    frames = lax.axis_size(FRAME)
    position = lax.axis_index(FRAME)
    columns = w_query.shape[1]
    rows, width = tokens.shape
    parts = lax.axis_size("x")
    here = lax.axis_index("x")
    depth = width // parts

    def columns_of(part):
        return lax.dynamic_slice_in_dim(tokens, part * depth, depth, 1)

    held = [columns_of(here)] + [swapped(columns_of(here ^ other), "x", other) for other in range(1, parts)]
    held = jnp.stack(held)
    ordered = [lax.dynamic_index_in_dim(held, here ^ part, 0, keepdims=False) for part in range(parts)]
    held = jnp.concatenate(ordered, axis=0)

    def summed(partial):
        received = lax.all_to_all(partial.reshape(parts, rows, -1), "x", 0, 0)
        return jnp.sum(received.astype(jnp.float32), axis=0)

    panel = lax.all_gather(jnp.concatenate([w_key, w_value], axis=1), ("z", "core"), axis=0, tiled=True)
    padded = jnp.pad(w_query, ((0, 0), (0, HEAD_DIM)))
    panel, padded, held = lax.optimization_barrier((panel, padded, held))
    query_panel = lax.all_gather(padded, ("z", "core"), axis=0, tiled=True)[:, :columns]

    def partial_of(panel):
        return jnp.dot(held, panel, preferred_element_type=jnp.float32).astype(jnp.bfloat16)

    pair = summed(partial_of(panel))
    key_full, value_full = pair[:, :columns], pair[:, columns:]
    key_total = summed_over(jnp.sum(key_full * key_full, axis=1)[None], "head")
    key_total, query_parts = lax.optimization_barrier((key_total, partial_of(query_panel)))
    key_normed = (key_full * scale_of(key_total)[0][:, None] * key_gain[None, :]).astype(jnp.bfloat16)
    paired = jnp.concatenate([key_normed, value_full.astype(jnp.bfloat16)], axis=1)

    query = summed(query_parts)
    blocks, query_scale = collect(paired, query, frames)
    query_scale = jnp.broadcast_to(query_scale[:, None], (rows, HEAD_DIM))
    met = jnp.asarray(tiles_met(frames), jnp.int32)
    own_row = lax.dynamic_slice_in_dim(key_tiles, position, 1, 0)
    met_here = lax.dynamic_slice_in_dim(met, position, 1, 0)
    usable = jnp.any(own_row[0, None, :] == met_here[0, :, None], axis=1).astype(jnp.int32)
    return attend(query, query_scale, query_gain, blocks, usable)


def solution(mesh):
    shape = (4, mesh.shape["frame"] // 8, 2, mesh.shape["head"])
    split = Mesh(mesh.devices.reshape(shape), FRAME + ("head",))
    return jax.shard_map(
        on_device,
        mesh=split,
        in_specs=(
            P(FRAME, None),
            P(FRAME, "head"),
            P(FRAME, "head"),
            P(FRAME, "head"),
            P("head"),
            P("head"),
            P(),
        ),
        out_specs=P(FRAME, "head"),
        check_vma=False,
    )
```

```python
import functools

import jax
import jax.numpy as jnp
from jax import lax
from jax.experimental import pallas as pl
from jax.experimental.pallas import tpu as pltpu
from jax.sharding import Mesh, PartitionSpec as P

HEAD_DIM = 128
HEADS = 24
TILE = 128
FRAME = ("x", "z", "core")


def swapped(value, axis, distance):
    count = lax.axis_size(axis)
    return lax.ppermute(value, axis, [(index, index ^ distance) for index in range(count)])


def chip_swap(frames, apart):
    starts = range(0, frames - 2 * apart, 2)
    there = [(tile, tile + 2 * apart + 1) for tile in starts]
    return there + [(back, tile) for tile, back in there]


def chip_relay(frames, apart):
    first = [(tile + 2 * apart, tile) for tile in range(0, frames - 2 * apart, 2)]
    second = [(tile, tile + 2 * apart) for tile in range(1, frames - 2 * apart, 2)]
    return first + second


def collect(paired, frames):
    def send(value, route):
        return lax.ppermute(value, FRAME, route)

    def traded(value):
        return send(value, [(tile, tile ^ 1) for tile in range(frames)])

    mate = traded(paired)
    far = send(paired, [(tile, (tile + frames // 2) % frames) for tile in range(frames)])
    both = jnp.concatenate([paired, mate], axis=0)
    two = send(both, chip_swap(frames, 2))
    one = send(both, chip_swap(frames, 1))
    eight = send(both, chip_swap(frames, 8))
    four = send(two, chip_relay(frames, 2))
    one, far = lax.optimization_barrier((one, far))
    crossed = traded(jnp.concatenate([one, two[:TILE], eight[:TILE], four[:TILE]], axis=0))
    return [
        (paired, 0), (mate, 0), (far, 0), (one, 1), (two, 1), (four, 1), (eight, 1),
        (crossed, 0), (crossed, 1), (crossed, 2), (crossed, 3), (crossed, 4),
    ]


def tiles_met(frames):
    table = []
    for tile in range(frames):
        chip, core = divmod(tile, 2)
        side = 1 - 2 * core

        def at(apart, parity):
            return 2 * (chip + apart) + parity if 0 <= chip + apart < frames // 2 else -2

        direct = [at(side * apart, core) for apart in (1, 2, 4, 8)]
        crossed = [at(-side, core), at(-side, 1 - core)]
        crossed += [at(-side * apart, core) for apart in (2, 8, 4)]
        table.append([tile, tile ^ 1, (tile + frames // 2) % frames] + direct + crossed)
    return table


def scale_of(total, gain):
    return lax.rsqrt(total / (HEADS * HEAD_DIM) + 1e-06)[:, None] * gain[None, :]


def attend_kernel(heads_here, places, usable, query, *refs):
    out = refs[-1]
    columns = heads_here * HEAD_DIM
    for head in range(heads_here):
        part = slice(head * HEAD_DIM, (head + 1) * HEAD_DIM)
        value_part = slice(columns + head * HEAD_DIM, columns + (head + 1) * HEAD_DIM)
        queries = query[:, part]
        scores = []
        for index, (block, row) in enumerate(places):
            score = lax.dot_general(
                queries, refs[block][row * TILE : (row + 1) * TILE, part], (((1,), (1,)), ((), ())),
                preferred_element_type=jnp.float32,
            ) * HEAD_DIM ** (-0.5)
            scores.append(jnp.where(usable[index] > 0, score, -jnp.inf))
        highest = jnp.max(functools.reduce(jnp.maximum, scores), axis=1, keepdims=True)
        raised = [jnp.exp(score - highest) for score in scores]
        total = jnp.sum(functools.reduce(jnp.add, raised), axis=1, keepdims=True)
        combined = jnp.zeros((TILE, HEAD_DIM), jnp.float32)
        for index, (block, row) in enumerate(places):
            combined += jnp.dot(
                raised[index].astype(jnp.bfloat16),
                refs[block][row * TILE : (row + 1) * TILE, value_part],
                preferred_element_type=jnp.float32,
            )
        out[:, part] = (combined / total).astype(out.dtype)


def attend(query, blocks, usable):
    arrays, places = [], []
    for array, row in blocks:
        known = [index for index, other in enumerate(arrays) if other is array]
        if not known:
            arrays.append(array)
        places.append((known[0] if known else len(arrays) - 1, row))
    rows, columns = query.shape
    heads_here = columns // HEAD_DIM
    count = len(blocks)
    vmem = pl.BlockSpec(memory_space=pltpu.VMEM)
    return pl.pallas_call(
        functools.partial(attend_kernel, heads_here, places),
        out_shape=jax.ShapeDtypeStruct((rows, columns), jnp.bfloat16),
        in_specs=[pl.BlockSpec(memory_space=pltpu.SMEM)] + [vmem] * (len(arrays) + 1),
        out_specs=vmem,
        compiler_params=pltpu.CompilerParams(vmem_limit_bytes=8 << 20),
        cost_estimate=pl.CostEstimate(
            flops=4 * rows * rows * columns * count,
            bytes_accessed=2 * rows * columns * (2 * count + 2),
            transcendentals=rows * rows * heads_here * count,
        ),
    )(usable, query, *arrays)


def on_device(tokens, w_query, w_key, w_value, query_gain, key_gain, key_tiles):
    frames = lax.axis_size(FRAME)
    position = lax.axis_index(FRAME)
    columns = w_query.shape[1]
    rows, width = tokens.shape
    parts = lax.axis_size("x")
    here = lax.axis_index("x")
    depth = width // parts

    panel = jnp.concatenate([w_key, w_value, w_query], axis=1)
    gathered = lax.all_gather(panel, ("z", "core"), axis=0, tiled=True)

    def columns_of(part):
        return lax.dynamic_slice_in_dim(tokens, part * depth, depth, 1)

    held = [columns_of(here)] + [swapped(columns_of(here ^ other), "x", other) for other in range(1, parts)]
    held = jnp.stack(held)
    ordered = [lax.dynamic_index_in_dim(held, here ^ part, 0, keepdims=False) for part in range(parts)]
    partial = jnp.dot(
        jnp.concatenate(ordered, axis=0), gathered, preferred_element_type=jnp.float32
    ).astype(jnp.bfloat16)
    partial = lax.all_to_all(partial.reshape(parts, rows, -1), "x", 0, 0)
    projected = jnp.sum(partial.astype(jnp.float32), axis=0)

    key_full = projected[:, :columns]
    value_full = projected[:, columns : 2 * columns]
    query = projected[:, 2 * columns :]
    squares = jnp.stack([jnp.sum(key_full * key_full, axis=1), jnp.sum(query * query, axis=1)])
    count = lax.axis_size("head")
    squares = lax.all_to_all(jnp.broadcast_to(squares[None], (count, 2, rows)), "head", 0, 0)
    totals = jnp.sum(squares, axis=0)
    key_normed = (key_full * scale_of(totals[0], key_gain)).astype(jnp.bfloat16)
    paired = jnp.concatenate([key_normed, value_full.astype(jnp.bfloat16)], axis=1)

    blocks = collect(paired, frames)
    met = jnp.asarray(tiles_met(frames), jnp.int32)
    own_row = lax.dynamic_slice_in_dim(key_tiles, position, 1, 0)
    met_here = lax.dynamic_slice_in_dim(met, position, 1, 0)
    usable = jnp.any(own_row[0, None, :] == met_here[0, :, None], axis=1).astype(jnp.int32)

    query_normed = (query * scale_of(totals[1], query_gain)).astype(jnp.bfloat16)
    return attend(query_normed, blocks, usable)


def solution(mesh):
    shape = (4, mesh.shape["frame"] // 8, 2, mesh.shape["head"])
    split = Mesh(mesh.devices.reshape(shape), FRAME + ("head",))
    return jax.shard_map(
        on_device,
        mesh=split,
        in_specs=(
            P(FRAME, None),
            P(FRAME, "head"),
            P(FRAME, "head"),
            P(FRAME, "head"),
            P("head"),
            P("head"),
            P(),
        ),
        out_specs=P(FRAME, "head"),
        check_vma=False,
    )
```

```python
import functools

import jax
import jax.numpy as jnp
from jax import lax
from jax.experimental import pallas as pl
from jax.experimental.pallas import tpu as pltpu
from jax.sharding import Mesh, PartitionSpec as P

HEAD_DIM = 128
HEADS = 24
TILE = 128
FRAME = ("x", "z", "core")


def swapped(value, axis, distance):
    count = lax.axis_size(axis)
    return lax.ppermute(value, axis, [(index, index ^ distance) for index in range(count)])


def chip_swap(frames, apart):
    starts = range(0, frames - 2 * apart, 2)
    there = [(tile, tile + 2 * apart + 1) for tile in starts]
    return there + [(back, tile) for tile, back in there]


def chip_relay(frames, apart):
    first = [(tile + 2 * apart, tile) for tile in range(0, frames - 2 * apart, 2)]
    second = [(tile, tile + 2 * apart) for tile in range(1, frames - 2 * apart, 2)]
    return first + second


def core_trade(value):
    return lax.ppermute(value, "core", [(0, 1), (1, 0)])


def collect(paired, mate, frames):
    def send(value, route):
        return lax.ppermute(value, FRAME, route)

    far = send(paired, [(tile, (tile + frames // 2) % frames) for tile in range(frames)])
    both = jnp.concatenate([paired, mate], axis=0)
    two = send(both, chip_swap(frames, 2))
    one = send(both, chip_swap(frames, 1))
    eight = send(both, chip_swap(frames, 8))
    four = send(two, chip_relay(frames, 2))
    one, far = lax.optimization_barrier((one, far))
    crossed = core_trade(jnp.concatenate([one, two[:TILE], eight[:TILE], four[:TILE]], axis=0))
    return [
        (paired, 0), (mate, 0), (far, 0), (one, 1), (two, 1), (four, 1), (eight, 1),
        (crossed, 0), (crossed, 1), (crossed, 2), (crossed, 3), (crossed, 4),
    ]


def tiles_met(frames):
    table = []
    for tile in range(frames):
        chip, core = divmod(tile, 2)
        side = 1 - 2 * core

        def at(apart, parity):
            return 2 * (chip + apart) + parity if 0 <= chip + apart < frames // 2 else -2

        direct = [at(side * apart, core) for apart in (1, 2, 4, 8)]
        crossed = [at(-side, core), at(-side, 1 - core)]
        crossed += [at(-side * apart, core) for apart in (2, 8, 4)]
        table.append([tile, tile ^ 1, (tile + frames // 2) % frames] + direct + crossed)
    return table


def scale_of(total):
    return lax.rsqrt(total / (HEADS * HEAD_DIM) + 1e-06)


def attend_kernel(heads_here, places, usable, query, *refs):
    out = refs[-1]
    columns = heads_here * HEAD_DIM
    for head in range(heads_here):
        part = slice(head * HEAD_DIM, (head + 1) * HEAD_DIM)
        value_part = slice(columns + head * HEAD_DIM, columns + (head + 1) * HEAD_DIM)
        queries = query[:, part]
        scores = []
        for index, (block, row) in enumerate(places):
            score = lax.dot_general(
                queries, refs[block][row * TILE : (row + 1) * TILE, part], (((1,), (1,)), ((), ())),
                preferred_element_type=jnp.float32,
            ) * HEAD_DIM ** (-0.5)
            scores.append(jnp.where(usable[index] > 0, score, -jnp.inf))
        highest = jnp.max(functools.reduce(jnp.maximum, scores), axis=1, keepdims=True)
        raised = [jnp.exp(score - highest) for score in scores]
        total = jnp.sum(functools.reduce(jnp.add, raised), axis=1, keepdims=True)
        combined = jnp.zeros((TILE, HEAD_DIM), jnp.float32)
        for index, (block, row) in enumerate(places):
            combined += jnp.dot(
                raised[index].astype(jnp.bfloat16),
                refs[block][row * TILE : (row + 1) * TILE, value_part],
                preferred_element_type=jnp.float32,
            )
        out[:, part] = (combined / total).astype(out.dtype)


def attend(query, blocks, usable):
    arrays, places = [], []
    for array, row in blocks:
        known = [index for index, other in enumerate(arrays) if other is array]
        if not known:
            arrays.append(array)
        places.append((known[0] if known else len(arrays) - 1, row))
    rows, columns = query.shape
    heads_here = columns // HEAD_DIM
    count = len(blocks)
    vmem = pl.BlockSpec(memory_space=pltpu.VMEM)
    return pl.pallas_call(
        functools.partial(attend_kernel, heads_here, places),
        out_shape=jax.ShapeDtypeStruct((rows, columns), jnp.bfloat16),
        in_specs=[pl.BlockSpec(memory_space=pltpu.SMEM)] + [vmem] * (len(arrays) + 1),
        out_specs=vmem,
        compiler_params=pltpu.CompilerParams(vmem_limit_bytes=8 << 20),
        cost_estimate=pl.CostEstimate(
            flops=4 * rows * rows * columns * count,
            bytes_accessed=2 * rows * columns * (2 * count + 2),
            transcendentals=rows * rows * heads_here * count,
        ),
    )(usable, query, *arrays)


def on_device(tokens, w_query, w_key, w_value, query_gain, key_gain, key_tiles):
    frames = lax.axis_size(FRAME)
    position = lax.axis_index(FRAME)
    columns = w_query.shape[1]
    rows, width = tokens.shape
    parts = lax.axis_size("x")
    here = lax.axis_index("x")
    depth = width // parts

    panel = jnp.concatenate([w_key, w_value, w_query], axis=1)
    gathered = lax.all_gather(panel, ("z", "core"), axis=0, tiled=True)

    def columns_of(part):
        return lax.dynamic_slice_in_dim(tokens, part * depth, depth, 1)

    held = [columns_of(here)] + [swapped(columns_of(here ^ other), "x", other) for other in range(1, parts)]
    held = jnp.stack(held)
    ordered = [lax.dynamic_index_in_dim(held, here ^ part, 0, keepdims=False) for part in range(parts)]
    partial = jnp.dot(
        jnp.concatenate(ordered, axis=0), gathered, preferred_element_type=jnp.float32
    ).astype(jnp.bfloat16)
    partial = lax.all_to_all(partial.reshape(parts, rows, -1), "x", 0, 0)
    projected = jnp.sum(partial.astype(jnp.float32), axis=0)

    key_full = projected[:, :columns]
    value_full = projected[:, columns : 2 * columns]
    query = projected[:, 2 * columns :]
    squares = jnp.stack([jnp.sum(key_full * key_full, axis=1), jnp.sum(query * query, axis=1)])

    cores, heads = lax.axis_size("core"), lax.axis_size("head")
    squares = jnp.broadcast_to(squares[None], (cores * heads, 2, rows))
    plain = projected[:, : 2 * columns].astype(jnp.bfloat16)
    mate_plain = core_trade(plain)
    totals = lax.all_to_all(squares, ("core", "head"), 0, 0).reshape(cores, heads, 2, rows).sum(axis=1)
    first_core = lax.axis_index("core") == 0
    own_scales = scale_of(jnp.where(first_core, totals[0], totals[1]))
    mate_scale = scale_of(jnp.where(first_core, totals[1, 0], totals[0, 0]))
    own_scales, mate_scale, mate_plain = lax.optimization_barrier((own_scales, mate_scale, mate_plain))

    def normed(keys, scale, gain):
        return (keys.astype(jnp.float32) * scale[:, None] * gain[None, :]).astype(jnp.bfloat16)

    paired = jnp.concatenate([normed(key_full, own_scales[0], key_gain), plain[:, columns:]], axis=1)
    mate = jnp.concatenate(
        [normed(mate_plain[:, :columns], mate_scale, key_gain), mate_plain[:, columns:]], axis=1
    )

    blocks = collect(paired, mate, frames)
    met = jnp.asarray(tiles_met(frames), jnp.int32)
    own_row = lax.dynamic_slice_in_dim(key_tiles, position, 1, 0)
    met_here = lax.dynamic_slice_in_dim(met, position, 1, 0)
    usable = jnp.any(own_row[0, None, :] == met_here[0, :, None], axis=1).astype(jnp.int32)

    query_normed = normed(query, own_scales[1], query_gain)
    return attend(query_normed, blocks, usable)


def solution(mesh):
    shape = (4, mesh.shape["frame"] // 8, 2, mesh.shape["head"])
    split = Mesh(mesh.devices.reshape(shape), FRAME + ("head",))
    return jax.shard_map(
        on_device,
        mesh=split,
        in_specs=(
            P(FRAME, None),
            P(FRAME, "head"),
            P(FRAME, "head"),
            P(FRAME, "head"),
            P("head"),
            P("head"),
            P(),
        ),
        out_specs=P(FRAME, "head"),
        check_vma=False,
    )
```

```python
import functools

import jax
import jax.numpy as jnp
from jax import lax
from jax.experimental import pallas as pl
from jax.experimental.pallas import tpu as pltpu
from jax.sharding import Mesh, PartitionSpec as P

HEAD_DIM = 128
HEADS = 24
TILE = 128
FRAME = ("x", "z", "core")


def swapped(value, axis, distance):
    count = lax.axis_size(axis)
    return lax.ppermute(value, axis, [(index, index ^ distance) for index in range(count)])


def chip_swap(frames, apart):
    starts = range(0, frames - 2 * apart, 2)
    there = [(tile, tile + 2 * apart + 1) for tile in starts]
    return there + [(back, tile) for tile, back in there]


def chip_relay(frames, apart):
    first = [(tile + 2 * apart, tile) for tile in range(0, frames - 2 * apart, 2)]
    second = [(tile, tile + 2 * apart) for tile in range(1, frames - 2 * apart, 2)]
    return first + second


def core_trade(value):
    return lax.ppermute(value, "core", [(0, 1), (1, 0)])


def collect(paired, mate, frames):
    def send(value, route):
        return lax.ppermute(value, FRAME, route)

    far = send(paired, [(tile, (tile + frames // 2) % frames) for tile in range(frames)])
    both = jnp.concatenate([paired, mate], axis=0)
    two = send(both, chip_swap(frames, 2))
    one = send(both, chip_swap(frames, 1))
    eight = send(both, chip_swap(frames, 8))
    four = send(two, chip_relay(frames, 2))
    one, far = lax.optimization_barrier((one, far))
    crossed = core_trade(jnp.concatenate([one, two[:TILE], eight[:TILE], four[:TILE]], axis=0))
    return [
        (paired, 0), (mate, 0), (far, 0), (one, 1), (two, 1), (four, 1), (eight, 1),
        (crossed, 0), (crossed, 1), (crossed, 2), (crossed, 3), (crossed, 4),
    ]


def tiles_met(frames):
    table = []
    for tile in range(frames):
        chip, core = divmod(tile, 2)
        side = 1 - 2 * core

        def at(apart, parity):
            return 2 * (chip + apart) + parity if 0 <= chip + apart < frames // 2 else -2

        direct = [at(side * apart, core) for apart in (1, 2, 4, 8)]
        crossed = [at(-side, core), at(-side, 1 - core)]
        crossed += [at(-side * apart, core) for apart in (2, 8, 4)]
        table.append([tile, tile ^ 1, (tile + frames // 2) % frames] + direct + crossed)
    return table


def scale_of(total):
    return lax.rsqrt(total / (HEADS * HEAD_DIM) + 1e-06)


def attend_kernel(heads_here, places, first, carried, last, usable, query, *refs):
    carry, refs = (refs[:3], refs[3:]) if carried else (None, refs)
    outs = refs[-1:] if last else refs[-3:]
    columns = heads_here * HEAD_DIM
    for head in range(heads_here):
        part = slice(head * HEAD_DIM, (head + 1) * HEAD_DIM)
        lane = slice(head * HEAD_DIM, head * HEAD_DIM + 1)
        value_part = slice(columns + head * HEAD_DIM, columns + (head + 1) * HEAD_DIM)
        queries = query[:, part]
        scores = []
        for index, (block, row) in enumerate(places):
            score = lax.dot_general(
                queries, refs[block][row * TILE : (row + 1) * TILE, part], (((1,), (1,)), ((), ())),
                preferred_element_type=jnp.float32,
            ) * HEAD_DIM ** (-0.5)
            scores.append(jnp.where(usable[first + index] > 0, score, -jnp.inf))
        highest = jnp.max(functools.reduce(jnp.maximum, scores), axis=1, keepdims=True)
        if carried:
            before = carry[1][:, lane]
            highest = jnp.maximum(highest, before)
            kept = jnp.exp(before - highest)
        raised = [jnp.exp(score - highest) for score in scores]
        total = jnp.sum(functools.reduce(jnp.add, raised), axis=1, keepdims=True)
        combined = jnp.zeros((TILE, HEAD_DIM), jnp.float32)
        if carried:
            total += carry[2][:, lane] * kept
            combined += carry[0][:, part] * kept
        for index, (block, row) in enumerate(places):
            combined += jnp.dot(
                raised[index].astype(jnp.bfloat16),
                refs[block][row * TILE : (row + 1) * TILE, value_part],
                preferred_element_type=jnp.float32,
            )
        if last:
            outs[0][:, part] = (combined / total).astype(outs[0].dtype)
        else:
            outs[0][:, part] = combined
            outs[1][:, part] = jnp.broadcast_to(highest, combined.shape)
            outs[2][:, part] = jnp.broadcast_to(total, combined.shape)


def attend(query, blocks, usable, first, carry):
    arrays, places = [], []
    for array, row in blocks:
        known = [index for index, other in enumerate(arrays) if other is array]
        if not known:
            arrays.append(array)
        places.append((known[0] if known else len(arrays) - 1, row))
    last = bool(carry)
    rows, columns = query.shape
    heads_here = columns // HEAD_DIM
    count = len(blocks)
    vmem = pl.BlockSpec(memory_space=pltpu.VMEM)
    running = [jax.ShapeDtypeStruct((rows, columns), jnp.float32)] * 3
    return pl.pallas_call(
        functools.partial(attend_kernel, heads_here, places, first, bool(carry), last),
        out_shape=jax.ShapeDtypeStruct((rows, columns), jnp.bfloat16) if last else running,
        in_specs=[pl.BlockSpec(memory_space=pltpu.SMEM)] + [vmem] * (len(carry) + len(arrays) + 1),
        out_specs=vmem if last else [vmem] * 3,
        compiler_params=pltpu.CompilerParams(vmem_limit_bytes=8 << 20),
        cost_estimate=pl.CostEstimate(
            flops=4 * rows * rows * columns * count,
            bytes_accessed=2 * rows * columns * (2 * count + 2),
            transcendentals=rows * rows * heads_here * count,
        ),
    )(usable, query, *carry, *arrays)


def on_device(tokens, w_query, w_key, w_value, query_gain, key_gain, key_tiles):
    frames = lax.axis_size(FRAME)
    position = lax.axis_index(FRAME)
    columns = w_query.shape[1]
    rows, width = tokens.shape
    parts = lax.axis_size("x")
    here = lax.axis_index("x")
    depth = width // parts

    panel = jnp.concatenate([w_key, w_value, w_query], axis=1)
    gathered = lax.all_gather(panel, ("z", "core"), axis=0, tiled=True)

    def columns_of(part):
        return lax.dynamic_slice_in_dim(tokens, part * depth, depth, 1)

    held = [columns_of(here)] + [swapped(columns_of(here ^ other), "x", other) for other in range(1, parts)]
    held = jnp.stack(held)
    ordered = [lax.dynamic_index_in_dim(held, here ^ part, 0, keepdims=False) for part in range(parts)]
    partial = jnp.dot(
        jnp.concatenate(ordered, axis=0), gathered, preferred_element_type=jnp.float32
    ).astype(jnp.bfloat16)
    partial = lax.all_to_all(partial.reshape(parts, rows, -1), "x", 0, 0)
    projected = jnp.sum(partial.astype(jnp.float32), axis=0)

    key_full = projected[:, :columns]
    value_full = projected[:, columns : 2 * columns]
    query = projected[:, 2 * columns :]
    squares = jnp.stack([jnp.sum(key_full * key_full, axis=1), jnp.sum(query * query, axis=1)])

    cores, heads = lax.axis_size("core"), lax.axis_size("head")
    squares = jnp.broadcast_to(squares[None], (cores * heads, 2, rows))
    plain = projected[:, : 2 * columns].astype(jnp.bfloat16)
    mate_plain = core_trade(plain)
    totals = lax.all_to_all(squares, ("core", "head"), 0, 0).reshape(cores, heads, 2, rows).sum(axis=1)
    first_core = lax.axis_index("core") == 0
    own_scales = scale_of(jnp.where(first_core, totals[0], totals[1]))
    mate_scale = scale_of(jnp.where(first_core, totals[1, 0], totals[0, 0]))
    met = jnp.asarray(tiles_met(frames), jnp.int32)
    own_row = lax.dynamic_slice_in_dim(key_tiles, position, 1, 0)
    met_here = lax.dynamic_slice_in_dim(met, position, 1, 0)
    usable = jnp.any(own_row[0, None, :] == met_here[0, :, None], axis=1).astype(jnp.int32)
    own_scales, mate_scale, mate_plain, usable = lax.optimization_barrier(
        (own_scales, mate_scale, mate_plain, usable)
    )

    def normed(keys, scale, gain):
        return (keys.astype(jnp.float32) * scale[:, None] * gain[None, :]).astype(jnp.bfloat16)

    paired = jnp.concatenate([normed(key_full, own_scales[0], key_gain), plain[:, columns:]], axis=1)
    mate = jnp.concatenate(
        [normed(mate_plain[:, :columns], mate_scale, key_gain), mate_plain[:, columns:]], axis=1
    )

    blocks = collect(paired, mate, frames)
    query_normed = normed(query, own_scales[1], query_gain)
    fetched, traded = blocks[:7], blocks[7:]
    running = attend(query_normed, fetched, usable, 0, ())
    return attend(query_normed, traded, usable, len(fetched), running)


def solution(mesh):
    shape = (4, mesh.shape["frame"] // 8, 2, mesh.shape["head"])
    split = Mesh(mesh.devices.reshape(shape), FRAME + ("head",))
    return jax.shard_map(
        on_device,
        mesh=split,
        in_specs=(
            P(FRAME, None),
            P(FRAME, "head"),
            P(FRAME, "head"),
            P(FRAME, "head"),
            P("head"),
            P("head"),
            P(),
        ),
        out_specs=P(FRAME, "head"),
        check_vma=False,
    )
```

```python
import functools

import jax
import jax.numpy as jnp
from jax import lax
from jax.experimental import pallas as pl
from jax.experimental.pallas import tpu as pltpu
from jax.sharding import Mesh, PartitionSpec as P

HEAD_DIM = 128
HEADS = 24
TILE = 128
FRAME = ("x", "z", "core")


def swapped(value, axis, distance):
    count = lax.axis_size(axis)
    return lax.ppermute(value, axis, [(index, index ^ distance) for index in range(count)])


def chip_swap(frames, apart):
    starts = range(0, frames - 2 * apart, 2)
    there = [(tile, tile + 2 * apart + 1) for tile in starts]
    return there + [(back, tile) for tile, back in there]


def chip_relay(frames, apart):
    first = [(tile + 2 * apart, tile) for tile in range(0, frames - 2 * apart, 2)]
    second = [(tile, tile + 2 * apart) for tile in range(1, frames - 2 * apart, 2)]
    return first + second


def core_trade(value):
    return lax.ppermute(value, "core", [(0, 1), (1, 0)])


def collect(paired, mate, frames):
    def send(value, route):
        return lax.ppermute(value, FRAME, route)

    far = send(paired, [(tile, (tile + frames // 2) % frames) for tile in range(frames)])
    both = jnp.concatenate([paired, mate], axis=0)
    two = send(both, chip_swap(frames, 2))
    one = send(both, chip_swap(frames, 1))
    eight = send(both, chip_swap(frames, 8))
    four = send(two, chip_relay(frames, 2))
    one, far = lax.optimization_barrier((one, far))
    crossed = core_trade(jnp.concatenate([one, two[:TILE], eight[:TILE], four[:TILE]], axis=0))
    return [
        (paired, 0), (mate, 0), (far, 0), (one, 1), (two, 1), (four, 1), (eight, 1),
        (crossed, 0), (crossed, 1), (crossed, 2), (crossed, 3), (crossed, 4),
    ]


def tiles_met(frames):
    table = []
    for tile in range(frames):
        chip, core = divmod(tile, 2)
        side = 1 - 2 * core

        def at(apart, parity):
            return 2 * (chip + apart) + parity if 0 <= chip + apart < frames // 2 else -2

        direct = [at(side * apart, core) for apart in (1, 2, 4, 8)]
        crossed = [at(-side, core), at(-side, 1 - core)]
        crossed += [at(-side * apart, core) for apart in (2, 8, 4)]
        table.append([tile, tile ^ 1, (tile + frames // 2) % frames] + direct + crossed)
    return table


def scale_of(total):
    return lax.rsqrt(total / (HEADS * HEAD_DIM) + 1e-06)


def attend_kernel(heads_here, places, first, carried, last, usable, query, *refs):
    carry, refs = (refs[:3], refs[3:]) if carried else (None, refs)
    outs = refs[-1:] if last else refs[-3:]
    columns = heads_here * HEAD_DIM
    heads = range(heads_here)
    part = [slice(head * HEAD_DIM, (head + 1) * HEAD_DIM) for head in heads]
    lane = [slice(head * HEAD_DIM, head * HEAD_DIM + 1) for head in heads]
    value_part = [slice(columns + head * HEAD_DIM, columns + (head + 1) * HEAD_DIM) for head in heads]

    def score_of(head, index, block, row):
        score = lax.dot_general(
            query[:, part[head]], refs[block][row * TILE : (row + 1) * TILE, part[head]],
            (((1,), (1,)), ((), ())), preferred_element_type=jnp.float32,
        ) * HEAD_DIM ** (-0.5)
        return jnp.where(usable[first + index] > 0, score, -jnp.inf)

    scores = [[score_of(head, index, *place) for index, place in enumerate(places)] for head in heads]
    highest = [jnp.max(functools.reduce(jnp.maximum, each), axis=1, keepdims=True) for each in scores]
    if carried:
        before = [carry[1][:, lane[head]] for head in heads]
        highest = [jnp.maximum(highest[head], before[head]) for head in heads]
        kept = [jnp.exp(before[head] - highest[head]) for head in heads]
    raised = [[jnp.exp(score - highest[head]) for score in scores[head]] for head in heads]
    total = [jnp.sum(functools.reduce(jnp.add, each), axis=1, keepdims=True) for each in raised]
    if carried:
        total = [total[head] + carry[2][:, lane[head]] * kept[head] for head in heads]
    for head in heads:
        combined = sum(
            jnp.dot(
                raised[head][index].astype(jnp.bfloat16),
                refs[block][row * TILE : (row + 1) * TILE, value_part[head]],
                preferred_element_type=jnp.float32,
            )
            for index, (block, row) in enumerate(places)
        )
        if carried:
            combined += carry[0][:, part[head]] * kept[head]
        if last:
            outs[0][:, part[head]] = (combined * (1.0 / total[head])).astype(outs[0].dtype)
        else:
            outs[0][:, part[head]] = combined
            outs[1][:, part[head]] = jnp.broadcast_to(highest[head], combined.shape)
            outs[2][:, part[head]] = jnp.broadcast_to(total[head], combined.shape)


def attend(query, blocks, usable, first, carry):
    arrays, places = [], []
    for array, row in blocks:
        known = [index for index, other in enumerate(arrays) if other is array]
        if not known:
            arrays.append(array)
        places.append((known[0] if known else len(arrays) - 1, row))
    last = bool(carry)
    rows, columns = query.shape
    heads_here = columns // HEAD_DIM
    count = len(blocks)
    vmem = pl.BlockSpec(memory_space=pltpu.VMEM)
    running = [jax.ShapeDtypeStruct((rows, columns), jnp.float32)] * 3
    return pl.pallas_call(
        functools.partial(attend_kernel, heads_here, places, first, bool(carry), last),
        out_shape=jax.ShapeDtypeStruct((rows, columns), jnp.bfloat16) if last else running,
        in_specs=[pl.BlockSpec(memory_space=pltpu.SMEM)] + [vmem] * (len(carry) + len(arrays) + 1),
        out_specs=vmem if last else [vmem] * 3,
        compiler_params=pltpu.CompilerParams(vmem_limit_bytes=8 << 20),
        cost_estimate=pl.CostEstimate(
            flops=4 * rows * rows * columns * count,
            bytes_accessed=2 * rows * columns * (2 * count + 2),
            transcendentals=rows * rows * heads_here * count,
        ),
    )(usable, query, *carry, *arrays)


def on_device(tokens, w_query, w_key, w_value, query_gain, key_gain, key_tiles):
    frames = lax.axis_size(FRAME)
    position = lax.axis_index(FRAME)
    columns = w_query.shape[1]
    rows, width = tokens.shape
    parts = lax.axis_size("x")
    here = lax.axis_index("x")
    depth = width // parts
    core = lax.axis_index("core")
    tokens, position, core = lax.optimization_barrier((tokens, position, core))

    panel = jnp.concatenate([w_key, w_value, w_query], axis=1)
    gathered = lax.all_gather(panel, ("z", "core"), axis=0, tiled=True)

    def columns_of(part):
        return lax.dynamic_slice_in_dim(tokens, part * depth, depth, 1)

    held = [columns_of(here)] + [swapped(columns_of(here ^ other), "x", other) for other in range(1, parts)]
    held = jnp.stack(held)
    ordered = [lax.dynamic_index_in_dim(held, here ^ part, 0, keepdims=False) for part in range(parts)]
    met = jnp.asarray(tiles_met(frames), jnp.int32)
    own_row = lax.dynamic_slice_in_dim(key_tiles, position, 1, 0)
    met_here = lax.dynamic_slice_in_dim(met, position, 1, 0)
    usable = jnp.any(own_row[0, None, :] == met_here[0, :, None], axis=1).astype(jnp.int32)
    held, usable, core = lax.optimization_barrier((jnp.concatenate(ordered, axis=0), usable, core))
    partial = jnp.dot(
        held, gathered, preferred_element_type=jnp.float32
    ).astype(jnp.bfloat16)
    partial = lax.all_to_all(partial.reshape(parts, rows, -1), "x", 0, 0)
    projected = jnp.sum(partial.astype(jnp.float32), axis=0)

    key_full = projected[:, :columns]
    value_full = projected[:, columns : 2 * columns]
    query = projected[:, 2 * columns :]
    squares = jnp.stack([jnp.sum(key_full * key_full, axis=1), jnp.sum(query * query, axis=1)])

    cores, heads = lax.axis_size("core"), lax.axis_size("head")
    squares = jnp.broadcast_to(squares[None], (cores * heads, 2, rows))
    plain = projected[:, : 2 * columns].astype(jnp.bfloat16)
    mate_plain = core_trade(plain)
    totals = lax.all_to_all(squares, ("core", "head"), 0, 0).reshape(cores, heads, 2, rows).sum(axis=1)
    first_core = core == 0
    own_scales = scale_of(jnp.where(first_core, totals[0], totals[1]))
    mate_scale = scale_of(jnp.where(first_core, totals[1, 0], totals[0, 0]))
    own_scales, mate_scale, mate_plain = lax.optimization_barrier((own_scales, mate_scale, mate_plain))

    def normed(keys, scale, gain):
        return (keys.astype(jnp.float32) * scale[:, None] * gain[None, :]).astype(jnp.bfloat16)

    paired = jnp.concatenate([normed(key_full, own_scales[0], key_gain), plain[:, columns:]], axis=1)
    mate = jnp.concatenate(
        [normed(mate_plain[:, :columns], mate_scale, key_gain), mate_plain[:, columns:]], axis=1
    )

    blocks = collect(paired, mate, frames)
    query_normed = normed(query, own_scales[1], query_gain)
    fetched, traded = blocks[:7], blocks[7:]
    running = attend(query_normed, fetched, usable, 0, ())
    return attend(query_normed, traded, usable, len(fetched), running)


def solution(mesh):
    shape = (4, mesh.shape["frame"] // 8, 2, mesh.shape["head"])
    split = Mesh(mesh.devices.reshape(shape), FRAME + ("head",))
    return jax.shard_map(
        on_device,
        mesh=split,
        in_specs=(
            P(FRAME, None),
            P(FRAME, "head"),
            P(FRAME, "head"),
            P(FRAME, "head"),
            P("head"),
            P("head"),
            P(),
        ),
        out_specs=P(FRAME, "head"),
        check_vma=False,
    )
```

```python
import functools

import jax
import jax.numpy as jnp
from jax import lax
from jax.experimental import pallas as pl
from jax.experimental.pallas import tpu as pltpu
from jax.sharding import Mesh, PartitionSpec as P

HEAD_DIM = 128
HEADS = 24
TILE = 128
FRAME = ("x", "z", "core")


def swapped(value, axis, distance):
    count = lax.axis_size(axis)
    return lax.ppermute(value, axis, [(index, index ^ distance) for index in range(count)])


def chip_swap(frames, apart):
    starts = range(0, frames - 2 * apart, 2)
    there = [(tile, tile + 2 * apart + 1) for tile in starts]
    return there + [(back, tile) for tile, back in there]


def chip_relay(frames, apart):
    first = [(tile + 2 * apart, tile) for tile in range(0, frames - 2 * apart, 2)]
    second = [(tile, tile + 2 * apart) for tile in range(1, frames - 2 * apart, 2)]
    return first + second


def core_trade(value):
    return lax.ppermute(value, "core", [(0, 1), (1, 0)])


def collect(paired, mate, frames):
    def send(value, route):
        return lax.ppermute(value, FRAME, route)

    far = send(paired, [(tile, (tile + frames // 2) % frames) for tile in range(frames)])
    both = jnp.concatenate([paired, mate], axis=0)
    two = send(both, chip_swap(frames, 2))
    one = send(both, chip_swap(frames, 1))
    eight = send(both, chip_swap(frames, 8))
    four = send(two, chip_relay(frames, 2))
    one, far = lax.optimization_barrier((one, far))
    crossed = core_trade(jnp.concatenate([one, two[:TILE], eight[:TILE], four[:TILE]], axis=0))
    return [
        (paired, 0), (mate, 0), (far, 0), (one, 1), (two, 1), (four, 1), (eight, 1),
        (crossed, 0), (crossed, 1), (crossed, 2), (crossed, 3), (crossed, 4),
    ]


def tiles_met(frames):
    table = []
    for tile in range(frames):
        chip, core = divmod(tile, 2)
        side = 1 - 2 * core

        def at(apart, parity):
            return 2 * (chip + apart) + parity if 0 <= chip + apart < frames // 2 else -2

        direct = [at(side * apart, core) for apart in (1, 2, 4, 8)]
        crossed = [at(-side, core), at(-side, 1 - core)]
        crossed += [at(-side * apart, core) for apart in (2, 8, 4)]
        table.append([tile, tile ^ 1, (tile + frames // 2) % frames] + direct + crossed)
    return table


def scale_of(total):
    return lax.rsqrt(total / (HEADS * HEAD_DIM) + 1e-06)


def attend_kernel(heads_here, places, first, carried, last, usable, query, *refs):
    carry, refs = (refs[:3], refs[3:]) if carried else (None, refs)
    outs = refs[-1:] if last else refs[-3:]
    columns = heads_here * HEAD_DIM
    heads = range(heads_here)
    part = [slice(head * HEAD_DIM, (head + 1) * HEAD_DIM) for head in heads]
    lane = [slice(head * HEAD_DIM, head * HEAD_DIM + 1) for head in heads]
    value_part = [slice(columns + head * HEAD_DIM, columns + (head + 1) * HEAD_DIM) for head in heads]

    def score_of(head, index, block, row):
        score = lax.dot_general(
            query[:, part[head]], refs[block][row * TILE : (row + 1) * TILE, part[head]],
            (((1,), (1,)), ((), ())), preferred_element_type=jnp.float32,
        ) * HEAD_DIM ** (-0.5)
        return jnp.where(usable[first + index] > 0, score, -jnp.inf)

    scores = [[score_of(head, index, *place) for index, place in enumerate(places)] for head in heads]
    highest = [jnp.max(functools.reduce(jnp.maximum, each), axis=1, keepdims=True) for each in scores]
    if carried:
        before = [carry[1][:, lane[head]] for head in heads]
        highest = [jnp.maximum(highest[head], before[head]) for head in heads]
        kept = [jnp.exp(before[head] - highest[head]) for head in heads]
    raised = [[jnp.exp(score - highest[head]) for score in scores[head]] for head in heads]
    total = [jnp.sum(functools.reduce(jnp.add, each), axis=1, keepdims=True) for each in raised]
    if carried:
        total = [total[head] + carry[2][:, lane[head]] * kept[head] for head in heads]
    for head in heads:
        combined = sum(
            jnp.dot(
                raised[head][index].astype(jnp.bfloat16),
                refs[block][row * TILE : (row + 1) * TILE, value_part[head]],
                preferred_element_type=jnp.float32,
            )
            for index, (block, row) in enumerate(places)
        )
        if carried:
            combined += carry[0][:, part[head]] * kept[head]
        if last:
            outs[0][:, part[head]] = (combined * (1.0 / total[head])).astype(outs[0].dtype)
        else:
            outs[0][:, part[head]] = combined
            outs[1][:, part[head]] = jnp.broadcast_to(highest[head], combined.shape)
            outs[2][:, part[head]] = jnp.broadcast_to(total[head], combined.shape)


def attend(query, blocks, usable, first, carry):
    arrays, places = [], []
    for array, row in blocks:
        known = [index for index, other in enumerate(arrays) if other is array]
        if not known:
            arrays.append(array)
        places.append((known[0] if known else len(arrays) - 1, row))
    last = bool(carry)
    rows, columns = query.shape
    heads_here = columns // HEAD_DIM
    count = len(blocks)
    vmem = pl.BlockSpec(memory_space=pltpu.VMEM)
    running = [jax.ShapeDtypeStruct((rows, columns), jnp.float32)] * 3
    return pl.pallas_call(
        functools.partial(attend_kernel, heads_here, places, first, bool(carry), last),
        out_shape=jax.ShapeDtypeStruct((rows, columns), jnp.bfloat16) if last else running,
        in_specs=[pl.BlockSpec(memory_space=pltpu.SMEM)] + [vmem] * (len(carry) + len(arrays) + 1),
        out_specs=vmem if last else [vmem] * 3,
        compiler_params=pltpu.CompilerParams(vmem_limit_bytes=8 << 20),
        cost_estimate=pl.CostEstimate(
            flops=4 * rows * rows * columns * count,
            bytes_accessed=2 * rows * columns * (2 * count + 2),
            transcendentals=rows * rows * heads_here * count,
        ),
    )(usable, query, *carry, *arrays)


def project_kernel(held, panel, out):
    columns = panel.shape[1]
    for start in range(0, columns, 256):
        chunk = slice(start, min(start + 256, columns))
        out[:, chunk] = jnp.dot(
            held[...], panel[:, chunk], preferred_element_type=jnp.float32
        ).astype(out.dtype)


def project(held, panel):
    rows, depth = held.shape
    columns = panel.shape[1]
    vmem = pl.BlockSpec(memory_space=pltpu.VMEM)
    return pl.pallas_call(
        project_kernel,
        out_shape=jax.ShapeDtypeStruct((rows, columns), jnp.bfloat16),
        in_specs=[vmem, vmem],
        out_specs=vmem,
        compiler_params=pltpu.CompilerParams(vmem_limit_bytes=10 << 20),
        cost_estimate=pl.CostEstimate(
            flops=2 * rows * depth * columns,
            bytes_accessed=2 * (rows * depth + depth * columns + rows * columns),
            transcendentals=0,
        ),
    )(held, panel)


def on_device(tokens, w_query, w_key, w_value, query_gain, key_gain, key_tiles):
    frames = lax.axis_size(FRAME)
    position = lax.axis_index(FRAME)
    columns = w_query.shape[1]
    rows, width = tokens.shape
    parts = lax.axis_size("x")
    here = lax.axis_index("x")
    depth = width // parts
    core = lax.axis_index("core")
    tokens, position, core = lax.optimization_barrier((tokens, position, core))

    panel = jnp.concatenate([w_key, w_value, w_query], axis=1)
    gathered = lax.all_gather(panel, ("z", "core"), axis=0, tiled=True)

    def columns_of(part):
        return lax.dynamic_slice_in_dim(tokens, part * depth, depth, 1)

    held = [columns_of(here)] + [swapped(columns_of(here ^ other), "x", other) for other in range(1, parts)]
    held = jnp.stack(held)
    ordered = [lax.dynamic_index_in_dim(held, here ^ part, 0, keepdims=False) for part in range(parts)]
    met = jnp.asarray(tiles_met(frames), jnp.int32)
    own_row = lax.dynamic_slice_in_dim(key_tiles, position, 1, 0)
    met_here = lax.dynamic_slice_in_dim(met, position, 1, 0)
    usable = jnp.any(own_row[0, None, :] == met_here[0, :, None], axis=1).astype(jnp.int32)
    held, usable, core = lax.optimization_barrier((jnp.concatenate(ordered, axis=0), usable, core))
    partial = project(held, gathered)
    partial = lax.all_to_all(partial.reshape(parts, rows, -1), "x", 0, 0)
    projected = jnp.sum(partial.astype(jnp.float32), axis=0)

    key_full = projected[:, :columns]
    value_full = projected[:, columns : 2 * columns]
    query = projected[:, 2 * columns :]
    squares = jnp.stack([jnp.sum(key_full * key_full, axis=1), jnp.sum(query * query, axis=1)])

    cores, heads = lax.axis_size("core"), lax.axis_size("head")
    squares = jnp.broadcast_to(squares[None], (cores * heads, 2, rows))
    plain = projected[:, : 2 * columns].astype(jnp.bfloat16)
    mate_plain = core_trade(plain)
    totals = lax.all_to_all(squares, ("core", "head"), 0, 0).reshape(cores, heads, 2, rows).sum(axis=1)
    first_core = core == 0
    own_scales = scale_of(jnp.where(first_core, totals[0], totals[1]))
    mate_scale = scale_of(jnp.where(first_core, totals[1, 0], totals[0, 0]))
    own_scales, mate_scale, mate_plain = lax.optimization_barrier((own_scales, mate_scale, mate_plain))

    def normed(keys, scale, gain):
        return (keys.astype(jnp.float32) * scale[:, None] * gain[None, :]).astype(jnp.bfloat16)

    paired = jnp.concatenate([normed(key_full, own_scales[0], key_gain), plain[:, columns:]], axis=1)
    mate = jnp.concatenate(
        [normed(mate_plain[:, :columns], mate_scale, key_gain), mate_plain[:, columns:]], axis=1
    )

    blocks = collect(paired, mate, frames)
    query_normed = normed(query, own_scales[1], query_gain)
    fetched, traded = blocks[:7], blocks[7:]
    running = attend(query_normed, fetched, usable, 0, ())
    return attend(query_normed, traded, usable, len(fetched), running)


def solution(mesh):
    shape = (4, mesh.shape["frame"] // 8, 2, mesh.shape["head"])
    split = Mesh(mesh.devices.reshape(shape), FRAME + ("head",))
    return jax.shard_map(
        on_device,
        mesh=split,
        in_specs=(
            P(FRAME, None),
            P(FRAME, "head"),
            P(FRAME, "head"),
            P(FRAME, "head"),
            P("head"),
            P("head"),
            P(),
        ),
        out_specs=P(FRAME, "head"),
        check_vma=False,
    )
```

```python
import functools

import jax
import jax.numpy as jnp
from jax import lax
from jax.experimental import pallas as pl
from jax.experimental.pallas import tpu as pltpu
from jax.sharding import Mesh, PartitionSpec as P

HEAD_DIM = 128
HEADS = 24
TILE = 128
FRAME = ("x", "z", "core")


def swapped(value, axis, distance):
    count = lax.axis_size(axis)
    return lax.ppermute(value, axis, [(index, index ^ distance) for index in range(count)])


def chip_swap(frames, apart):
    starts = range(0, frames - 2 * apart, 2)
    there = [(tile, tile + 2 * apart + 1) for tile in starts]
    return there + [(back, tile) for tile, back in there]


def chip_relay(frames, apart):
    first = [(tile + 2 * apart, tile) for tile in range(0, frames - 2 * apart, 2)]
    second = [(tile, tile + 2 * apart) for tile in range(1, frames - 2 * apart, 2)]
    return first + second


def core_trade(value):
    return lax.ppermute(value, "core", [(0, 1), (1, 0)])


def collect(paired, mate, frames):
    def send(value, route):
        return lax.ppermute(value, FRAME, route)

    far = send(paired, [(tile, (tile + frames // 2) % frames) for tile in range(frames)])
    both = jnp.concatenate([paired, mate], axis=0)
    two = send(both, chip_swap(frames, 2))
    one = send(both, chip_swap(frames, 1))
    eight = send(both, chip_swap(frames, 8))
    four = send(two, chip_relay(frames, 2))
    one, far = lax.optimization_barrier((one, far))
    crossed = core_trade(jnp.concatenate([one, two[:TILE], eight[:TILE], four[:TILE]], axis=0))
    return [
        (paired, 0), (mate, 0), (far, 0), (one, 1), (two, 1), (four, 1), (eight, 1),
        (crossed, 0), (crossed, 1), (crossed, 2), (crossed, 3), (crossed, 4),
    ]


def tiles_met(frames):
    table = []
    for tile in range(frames):
        chip, core = divmod(tile, 2)
        side = 1 - 2 * core

        def at(apart, parity):
            return 2 * (chip + apart) + parity if 0 <= chip + apart < frames // 2 else -2

        direct = [at(side * apart, core) for apart in (1, 2, 4, 8)]
        crossed = [at(-side, core), at(-side, 1 - core)]
        crossed += [at(-side * apart, core) for apart in (2, 8, 4)]
        table.append([tile, tile ^ 1, (tile + frames // 2) % frames] + direct + crossed)
    return table


def scale_of(total):
    return lax.rsqrt(total / (HEADS * HEAD_DIM) + 1e-06)


def attend_kernel(heads_here, places, first, carried, last, usable, query, *refs):
    carry, refs = (refs[:3], refs[3:]) if carried else (None, refs)
    outs = refs[-1:] if last else refs[-3:]
    columns = heads_here * HEAD_DIM
    heads = range(heads_here)
    part = [slice(head * HEAD_DIM, (head + 1) * HEAD_DIM) for head in heads]
    lane = [slice(head * HEAD_DIM, head * HEAD_DIM + 1) for head in heads]
    value_part = [slice(columns + head * HEAD_DIM, columns + (head + 1) * HEAD_DIM) for head in heads]

    def score_of(head, index, block, row):
        score = lax.dot_general(
            query[:, part[head]], refs[block][row * TILE : (row + 1) * TILE, part[head]],
            (((1,), (1,)), ((), ())), preferred_element_type=jnp.float32,
        ) * HEAD_DIM ** (-0.5)
        return jnp.where(usable[first + index] > 0, score, -jnp.inf)

    scores = [[score_of(head, index, *place) for index, place in enumerate(places)] for head in heads]
    highest = [jnp.max(functools.reduce(jnp.maximum, each), axis=1, keepdims=True) for each in scores]
    if carried:
        before = [carry[1][:, lane[head]] for head in heads]
        highest = [jnp.maximum(highest[head], before[head]) for head in heads]
        kept = [jnp.exp(before[head] - highest[head]) for head in heads]
    raised = [[jnp.exp(score - highest[head]) for score in scores[head]] for head in heads]
    total = [jnp.sum(functools.reduce(jnp.add, each), axis=1, keepdims=True) for each in raised]
    if carried:
        total = [total[head] + carry[2][:, lane[head]] * kept[head] for head in heads]
    for head in heads:
        combined = sum(
            jnp.dot(
                raised[head][index].astype(jnp.bfloat16),
                refs[block][row * TILE : (row + 1) * TILE, value_part[head]],
                preferred_element_type=jnp.float32,
            )
            for index, (block, row) in enumerate(places)
        )
        if carried:
            combined += carry[0][:, part[head]] * kept[head]
        if last:
            outs[0][:, part[head]] = (combined * (1.0 / total[head])).astype(outs[0].dtype)
        else:
            outs[0][:, part[head]] = combined
            outs[1][:, part[head]] = jnp.broadcast_to(highest[head], combined.shape)
            outs[2][:, part[head]] = jnp.broadcast_to(total[head], combined.shape)


def attend(query, blocks, usable, first, carry):
    arrays, places = [], []
    for array, row in blocks:
        known = [index for index, other in enumerate(arrays) if other is array]
        if not known:
            arrays.append(array)
        places.append((known[0] if known else len(arrays) - 1, row))
    last = bool(carry)
    rows, columns = query.shape
    heads_here = columns // HEAD_DIM
    count = len(blocks)
    vmem = pl.BlockSpec(memory_space=pltpu.VMEM)
    running = [jax.ShapeDtypeStruct((rows, columns), jnp.float32)] * 3
    return pl.pallas_call(
        functools.partial(attend_kernel, heads_here, places, first, bool(carry), last),
        out_shape=jax.ShapeDtypeStruct((rows, columns), jnp.bfloat16) if last else running,
        in_specs=[pl.BlockSpec(memory_space=pltpu.SMEM)] + [vmem] * (len(carry) + len(arrays) + 1),
        out_specs=vmem if last else [vmem] * 3,
        compiler_params=pltpu.CompilerParams(vmem_limit_bytes=8 << 20),
        cost_estimate=pl.CostEstimate(
            flops=4 * rows * rows * columns * count,
            bytes_accessed=2 * rows * columns * (2 * count + 2),
            transcendentals=rows * rows * heads_here * count,
        ),
    )(usable, query, *carry, *arrays)


def project_kernel(chunks, held, panel, out, staged, arrived):
    copies = [
        pltpu.make_async_copy(panel.at[:, chunk], staged.at[:, chunk], arrived.at[index])
        for index, chunk in enumerate(chunks)
    ]
    for copy in copies:
        copy.start()
    for copy, chunk in zip(copies, chunks):
        copy.wait()
        out[:, chunk] = jnp.dot(
            held[...], staged[:, chunk], preferred_element_type=jnp.float32
        ).astype(out.dtype)


def project(held, panel):
    rows, depth = held.shape
    columns = panel.shape[1]
    chunks = [slice(start, min(start + 256, columns)) for start in range(0, columns, 256)]
    vmem = pl.BlockSpec(memory_space=pltpu.VMEM)
    return pl.pallas_call(
        functools.partial(project_kernel, chunks),
        out_shape=jax.ShapeDtypeStruct((rows, columns), jnp.bfloat16),
        in_specs=[vmem, pl.BlockSpec(memory_space=pltpu.HBM)],
        out_specs=vmem,
        scratch_shapes=[
            pltpu.VMEM(panel.shape, panel.dtype),
            pltpu.SemaphoreType.DMA((len(chunks),)),
        ],
        compiler_params=pltpu.CompilerParams(vmem_limit_bytes=50 << 20),
        cost_estimate=pl.CostEstimate(
            flops=2 * rows * depth * columns,
            bytes_accessed=2 * (rows * depth + depth * columns + rows * columns),
            transcendentals=0,
        ),
    )(held, panel)


def on_device(tokens, w_query, w_key, w_value, query_gain, key_gain, key_tiles):
    frames = lax.axis_size(FRAME)
    position = lax.axis_index(FRAME)
    columns = w_query.shape[1]
    rows, width = tokens.shape
    parts = lax.axis_size("x")
    here = lax.axis_index("x")
    depth = width // parts
    core = lax.axis_index("core")
    tokens, position, core = lax.optimization_barrier((tokens, position, core))

    panel = jnp.concatenate([w_key, w_value, w_query], axis=1)
    gathered = lax.all_gather(panel, ("z", "core"), axis=0, tiled=True)

    def columns_of(part):
        return lax.dynamic_slice_in_dim(tokens, part * depth, depth, 1)

    held = [columns_of(here)] + [swapped(columns_of(here ^ other), "x", other) for other in range(1, parts)]
    held = jnp.stack(held)
    ordered = [lax.dynamic_index_in_dim(held, here ^ part, 0, keepdims=False) for part in range(parts)]
    met = jnp.asarray(tiles_met(frames), jnp.int32)
    own_row = lax.dynamic_slice_in_dim(key_tiles, position, 1, 0)
    met_here = lax.dynamic_slice_in_dim(met, position, 1, 0)
    usable = jnp.any(own_row[0, None, :] == met_here[0, :, None], axis=1).astype(jnp.int32)
    held, usable, core = lax.optimization_barrier((jnp.concatenate(ordered, axis=0), usable, core))
    partial = project(held, gathered)
    partial = lax.all_to_all(partial.reshape(parts, rows, -1), "x", 0, 0)
    projected = jnp.sum(partial.astype(jnp.float32), axis=0)

    key_full = projected[:, :columns]
    value_full = projected[:, columns : 2 * columns]
    query = projected[:, 2 * columns :]
    squares = jnp.stack([jnp.sum(key_full * key_full, axis=1), jnp.sum(query * query, axis=1)])

    cores, heads = lax.axis_size("core"), lax.axis_size("head")
    squares = jnp.broadcast_to(squares[None], (cores * heads, 2, rows))
    plain = projected[:, : 2 * columns].astype(jnp.bfloat16)
    mate_plain = core_trade(plain)
    totals = lax.all_to_all(squares, ("core", "head"), 0, 0).reshape(cores, heads, 2, rows).sum(axis=1)
    first_core = core == 0
    own_scales = scale_of(jnp.where(first_core, totals[0], totals[1]))
    mate_scale = scale_of(jnp.where(first_core, totals[1, 0], totals[0, 0]))
    own_scales, mate_scale, mate_plain = lax.optimization_barrier((own_scales, mate_scale, mate_plain))

    def normed(keys, scale, gain):
        return (keys.astype(jnp.float32) * scale[:, None] * gain[None, :]).astype(jnp.bfloat16)

    paired = jnp.concatenate([normed(key_full, own_scales[0], key_gain), plain[:, columns:]], axis=1)
    mate = jnp.concatenate(
        [normed(mate_plain[:, :columns], mate_scale, key_gain), mate_plain[:, columns:]], axis=1
    )

    blocks = collect(paired, mate, frames)
    query_normed = normed(query, own_scales[1], query_gain)
    fetched, traded = blocks[:7], blocks[7:]
    running = attend(query_normed, fetched, usable, 0, ())
    return attend(query_normed, traded, usable, len(fetched), running)


def solution(mesh):
    shape = (4, mesh.shape["frame"] // 8, 2, mesh.shape["head"])
    split = Mesh(mesh.devices.reshape(shape), FRAME + ("head",))
    return jax.shard_map(
        on_device,
        mesh=split,
        in_specs=(
            P(FRAME, None),
            P(FRAME, "head"),
            P(FRAME, "head"),
            P(FRAME, "head"),
            P("head"),
            P("head"),
            P(),
        ),
        out_specs=P(FRAME, "head"),
        check_vma=False,
    )
```

```python
import functools

import jax
import jax.numpy as jnp
from jax import lax
from jax.experimental import pallas as pl
from jax.experimental.pallas import tpu as pltpu
from jax.sharding import Mesh, PartitionSpec as P

HEAD_DIM = 128
HEADS = 24
TILE = 128
FRAME = ("x", "z", "core")


def swapped(value, axis, distance):
    count = lax.axis_size(axis)
    return lax.ppermute(value, axis, [(index, index ^ distance) for index in range(count)])


def chip_swap(frames, apart):
    starts = range(0, frames - 2 * apart, 2)
    there = [(tile, tile + 2 * apart + 1) for tile in starts]
    return there + [(back, tile) for tile, back in there]


def chip_relay(frames, apart):
    first = [(tile + 2 * apart, tile) for tile in range(0, frames - 2 * apart, 2)]
    second = [(tile, tile + 2 * apart) for tile in range(1, frames - 2 * apart, 2)]
    return first + second


def core_trade(value):
    return lax.ppermute(value, "core", [(0, 1), (1, 0)])


def collect(paired, mate, frames):
    def send(value, route):
        return lax.ppermute(value, FRAME, route)

    far = send(paired, [(tile, (tile + frames // 2) % frames) for tile in range(frames)])
    both = jnp.concatenate([paired, mate], axis=0)
    two = send(both, chip_swap(frames, 2))
    one = send(both, chip_swap(frames, 1))
    eight = send(both, chip_swap(frames, 8))
    four = send(two, chip_relay(frames, 2))
    one, far = lax.optimization_barrier((one, far))
    crossed = core_trade(jnp.concatenate([one, two[:TILE], eight[:TILE], four[:TILE]], axis=0))
    return [
        (paired, 0), (mate, 0), (far, 0), (one, 1), (two, 1), (four, 1), (eight, 1),
        (crossed, 0), (crossed, 1), (crossed, 2), (crossed, 3), (crossed, 4),
    ]


def tiles_met(frames):
    table = []
    for tile in range(frames):
        chip, core = divmod(tile, 2)
        side = 1 - 2 * core

        def at(apart, parity):
            return 2 * (chip + apart) + parity if 0 <= chip + apart < frames // 2 else -2

        direct = [at(side * apart, core) for apart in (1, 2, 4, 8)]
        crossed = [at(-side, core), at(-side, 1 - core)]
        crossed += [at(-side * apart, core) for apart in (2, 8, 4)]
        table.append([tile, tile ^ 1, (tile + frames // 2) % frames] + direct + crossed)
    return table


def scale_of(total):
    return lax.rsqrt(total / (HEADS * HEAD_DIM) + 1e-06)


def attend_kernel(heads_here, places, first, carried, last, usable, query, *refs):
    carry, refs = (refs[:3], refs[3:]) if carried else (None, refs)
    outs = refs[-1:] if last else refs[-3:]
    columns = heads_here * HEAD_DIM
    heads = range(heads_here)
    part = [slice(head * HEAD_DIM, (head + 1) * HEAD_DIM) for head in heads]
    lane = [slice(head * HEAD_DIM, head * HEAD_DIM + 1) for head in heads]
    value_part = [slice(columns + head * HEAD_DIM, columns + (head + 1) * HEAD_DIM) for head in heads]

    def score_of(head, index, block, row):
        score = lax.dot_general(
            query[:, part[head]], refs[block][row * TILE : (row + 1) * TILE, part[head]],
            (((1,), (1,)), ((), ())), preferred_element_type=jnp.float32,
        ) * HEAD_DIM ** (-0.5)
        return jnp.where(usable[first + index] > 0, score, -jnp.inf)

    scores = [[score_of(head, index, *place) for index, place in enumerate(places)] for head in heads]
    highest = [jnp.max(functools.reduce(jnp.maximum, each), axis=1, keepdims=True) for each in scores]
    if carried:
        before = [carry[1][:, lane[head]] for head in heads]
        highest = [jnp.maximum(highest[head], before[head]) for head in heads]
        kept = [jnp.exp(before[head] - highest[head]) for head in heads]
    raised = [[jnp.exp(score - highest[head]) for score in scores[head]] for head in heads]
    total = [jnp.sum(functools.reduce(jnp.add, each), axis=1, keepdims=True) for each in raised]
    if carried:
        total = [total[head] + carry[2][:, lane[head]] * kept[head] for head in heads]
    for head in heads:
        combined = sum(
            jnp.dot(
                raised[head][index].astype(jnp.bfloat16),
                refs[block][row * TILE : (row + 1) * TILE, value_part[head]],
                preferred_element_type=jnp.float32,
            )
            for index, (block, row) in enumerate(places)
        )
        if carried:
            combined += carry[0][:, part[head]] * kept[head]
        if last:
            outs[0][:, part[head]] = (combined * (1.0 / total[head])).astype(outs[0].dtype)
        else:
            outs[0][:, part[head]] = combined
            outs[1][:, part[head]] = jnp.broadcast_to(highest[head], combined.shape)
            outs[2][:, part[head]] = jnp.broadcast_to(total[head], combined.shape)


def attend(query, blocks, usable, first, carry):
    arrays, places = [], []
    for array, row in blocks:
        known = [index for index, other in enumerate(arrays) if other is array]
        if not known:
            arrays.append(array)
        places.append((known[0] if known else len(arrays) - 1, row))
    last = bool(carry)
    rows, columns = query.shape
    heads_here = columns // HEAD_DIM
    count = len(blocks)
    vmem = pl.BlockSpec(memory_space=pltpu.VMEM)
    running = [jax.ShapeDtypeStruct((rows, columns), jnp.float32)] * 3
    return pl.pallas_call(
        functools.partial(attend_kernel, heads_here, places, first, bool(carry), last),
        out_shape=jax.ShapeDtypeStruct((rows, columns), jnp.bfloat16) if last else running,
        in_specs=[pl.BlockSpec(memory_space=pltpu.SMEM)] + [vmem] * (len(carry) + len(arrays) + 1),
        out_specs=vmem if last else [vmem] * 3,
        compiler_params=pltpu.CompilerParams(vmem_limit_bytes=8 << 20),
        cost_estimate=pl.CostEstimate(
            flops=4 * rows * rows * columns * count,
            bytes_accessed=2 * rows * columns * (2 * count + 2),
            transcendentals=rows * rows * heads_here * count,
        ),
    )(usable, query, *carry, *arrays)


def project_kernel(chunks, held, panel, out, staged, arrived):
    depth = panel.shape[0]
    copies = [
        pltpu.make_async_copy(panel.at[pl.ds(start, 160)], staged.at[pl.ds(start, 160)], arrived.at[index])
        for index, start in enumerate(range(0, depth, 160))
    ]
    for copy in copies:
        copy.start()
    for copy in copies:
        copy.wait()
    for chunk in chunks:
        out[:, chunk] = jnp.dot(
            held[...], staged[:, chunk], preferred_element_type=jnp.float32
        ).astype(out.dtype)


def project(held, panel):
    rows, depth = held.shape
    columns = panel.shape[1]
    chunks = [slice(start, min(start + 256, columns)) for start in range(0, columns, 256)]
    vmem = pl.BlockSpec(memory_space=pltpu.VMEM)
    return pl.pallas_call(
        functools.partial(project_kernel, chunks),
        out_shape=jax.ShapeDtypeStruct((rows, columns), jnp.bfloat16),
        in_specs=[vmem, pl.BlockSpec(memory_space=pltpu.HBM)],
        out_specs=vmem,
        scratch_shapes=[
            pltpu.VMEM(panel.shape, panel.dtype),
            pltpu.SemaphoreType.DMA((depth // 160,)),
        ],
        compiler_params=pltpu.CompilerParams(vmem_limit_bytes=50 << 20),
        cost_estimate=pl.CostEstimate(
            flops=2 * rows * depth * columns,
            bytes_accessed=2 * (rows * depth + depth * columns + rows * columns),
            transcendentals=0,
        ),
    )(held, panel)


def on_device(tokens, w_query, w_key, w_value, query_gain, key_gain, key_tiles):
    frames = lax.axis_size(FRAME)
    position = lax.axis_index(FRAME)
    columns = w_query.shape[1]
    rows, width = tokens.shape
    parts = lax.axis_size("x")
    here = lax.axis_index("x")
    depth = width // parts
    core = lax.axis_index("core")
    tokens, position, core = lax.optimization_barrier((tokens, position, core))

    panel = jnp.concatenate([w_key, w_value, w_query], axis=1)
    gathered = lax.all_gather(panel, ("z", "core"), axis=0, tiled=True)

    def columns_of(part):
        return lax.dynamic_slice_in_dim(tokens, part * depth, depth, 1)

    held = [columns_of(here)] + [swapped(columns_of(here ^ other), "x", other) for other in range(1, parts)]
    held = jnp.stack(held)
    ordered = [lax.dynamic_index_in_dim(held, here ^ part, 0, keepdims=False) for part in range(parts)]
    met = jnp.asarray(tiles_met(frames), jnp.int32)
    own_row = lax.dynamic_slice_in_dim(key_tiles, position, 1, 0)
    met_here = lax.dynamic_slice_in_dim(met, position, 1, 0)
    usable = jnp.any(own_row[0, None, :] == met_here[0, :, None], axis=1).astype(jnp.int32)
    held, usable, core = lax.optimization_barrier((jnp.concatenate(ordered, axis=0), usable, core))
    partial = project(held, gathered)
    partial = lax.all_to_all(partial.reshape(parts, rows, -1), "x", 0, 0)
    projected = jnp.sum(partial.astype(jnp.float32), axis=0)

    key_full = projected[:, :columns]
    value_full = projected[:, columns : 2 * columns]
    query = projected[:, 2 * columns :]
    squares = jnp.stack([jnp.sum(key_full * key_full, axis=1), jnp.sum(query * query, axis=1)])

    cores, heads = lax.axis_size("core"), lax.axis_size("head")
    squares = jnp.broadcast_to(squares[None], (cores * heads, 2, rows))
    plain = projected[:, : 2 * columns].astype(jnp.bfloat16)
    mate_plain = core_trade(plain)
    totals = lax.all_to_all(squares, ("core", "head"), 0, 0).reshape(cores, heads, 2, rows).sum(axis=1)
    first_core = core == 0
    own_scales = scale_of(jnp.where(first_core, totals[0], totals[1]))
    mate_scale = scale_of(jnp.where(first_core, totals[1, 0], totals[0, 0]))
    own_scales, mate_scale, mate_plain = lax.optimization_barrier((own_scales, mate_scale, mate_plain))

    def normed(keys, scale, gain):
        return (keys.astype(jnp.float32) * scale[:, None] * gain[None, :]).astype(jnp.bfloat16)

    paired = jnp.concatenate([normed(key_full, own_scales[0], key_gain), plain[:, columns:]], axis=1)
    mate = jnp.concatenate(
        [normed(mate_plain[:, :columns], mate_scale, key_gain), mate_plain[:, columns:]], axis=1
    )

    blocks = collect(paired, mate, frames)
    query_normed = normed(query, own_scales[1], query_gain)
    fetched, traded = blocks[:7], blocks[7:]
    running = attend(query_normed, fetched, usable, 0, ())
    return attend(query_normed, traded, usable, len(fetched), running)


def solution(mesh):
    shape = (4, mesh.shape["frame"] // 8, 2, mesh.shape["head"])
    split = Mesh(mesh.devices.reshape(shape), FRAME + ("head",))
    return jax.shard_map(
        on_device,
        mesh=split,
        in_specs=(
            P(FRAME, None),
            P(FRAME, "head"),
            P(FRAME, "head"),
            P(FRAME, "head"),
            P("head"),
            P("head"),
            P(),
        ),
        out_specs=P(FRAME, "head"),
        check_vma=False,
    )
```
